512 devices in a mesh: segment: 4 (over x), dp: 128 (over y, z, core).
Axes of the slice: x: 4, y: 8, z: 8, core: 2. Of those that a mesh axis runs over, the one named last changes fastest.
Arguments:
- fwd_in: bfloat16 [2, 4, 128, 16, 32, 256], P(None, 'segment', 'dp'), may hold values from -6 to 6
- bwd_in: bfloat16 [4, 4, 128, 16, 32, 256], P(None, 'segment', 'dp'), may hold values from -6 to 6
- fresh: bfloat16 [2, 128, 16, 32, 256], P(None, 'dp'), may hold values from -6 to 6
- top_cot: bfloat16 [2, 128, 16, 32, 256], P(None, 'dp'), may hold values from -6 to 6
- conv_weight: bfloat16 [4, 256, 9, 256], P('segment', 'dp'), may hold values from -0.125 to 0.125
Outputs:
- fwd_out: bfloat16 [2, 4, 128, 16, 32, 256], P(None, 'segment', 'dp')
- bwd_out: bfloat16 [4, 4, 128, 16, 32, 256], P(None, 'segment', 'dp')
- weight_grad: float32 [4, 256, 9, 256], P('segment', 'dp')
The draws below stay inside these ranges and needn't reach their ends.
All inputs are finite; a program needn't handle non-finite values.
Results may differ from the reference program's by a relative error of at most 0.0055.
Values may be sent and summed in bfloat16 or wider, within the bound.
A program may use at most 64 MiB of HBM per device.

```python
import jax
import jax.numpy as jnp
from jax import lax

C = 256
ROWS = 16
COLS = 32
SEGMENTS = 4
TILES = 128
PIXELS = 65536


def block_scale(rng, shape, shards, smallest, largest):
    factor_of = 1.0
    for position, parts in shards:
        heights = jax.random.uniform(jax.random.fold_in(jax.random.fold_in(rng, 6), position), (parts,), jnp.float32, smallest / len(shards), largest / len(shards))
        factor_of = factor_of * jnp.repeat(jnp.exp(heights), shape[position] // parts).reshape((-1,) + (1,) * (len(shape) - 1 - position))
    return factor_of


def gaussian(own_key, dims, scale, most, cuts=(), kind=jnp.bfloat16):
    entries = jax.random.normal(own_key, dims, jnp.float32) * scale
    if len(cuts) > 0:
        entries = block_scale(own_key, dims, cuts, -0.22, 0.18) * entries
    return jnp.clip(entries, min=-most, max=most).astype(kind)


def setup_inputs(seed: int = 0) -> dict:
    seeds = jax.random.split(jax.random.key(seed), 6)
    return {
        "fwd_in": gaussian(seeds[0], (2, SEGMENTS, TILES, ROWS, COLS, C), 1.0, 6.0, ((1, 4), (2, 128))),
        "bwd_in": gaussian(seeds[1], (4, SEGMENTS, TILES, ROWS, COLS, C), 1.0, 6.0, ((1, 4), (2, 128))),
        "fresh": gaussian(seeds[2], (2, TILES, ROWS, COLS, C), 1.0, 6.0, ((1, 128),)),
        "top_cot": gaussian(seeds[3], (2, TILES, ROWS, COLS, C), 1.0, 6.0, ((1, 128),)),
        "conv_weight": gaussian(seeds[4], (SEGMENTS, C, 9, C), (9 * C) ** -0.5, 0.125, ((0, 4), (1, 128))),
    }


def to_images(tiles):
    return tiles.reshape(tiles.shape[0] // 2, 2 * tiles.shape[1], tiles.shape[2], tiles.shape[3])


def to_tiles(images):
    return images.reshape(images.shape[0] * 2, images.shape[1] // 2, images.shape[2], images.shape[3])


def extended_of(images):
    return jnp.pad(images, ((0, 0), (1, 1), (1, 1), (0, 0)))


def conv_forward(extended, weight):
    height = extended.shape[1] - 2
    width = extended.shape[2] - 2
    channels = extended.shape[3]
    running = jnp.zeros((extended.shape[0] * height * width, weight.shape[2]), jnp.float32)
    for row_off in range(3):
        for col_off in range(3):
            window = extended[:, row_off:row_off + height, col_off:col_off + width, :].reshape(-1, channels)
            running = running + jnp.dot(window, weight[:, 3 * row_off + col_off, :], preferred_element_type=jnp.float32)
    return running.reshape(extended.shape[0], height, width, weight.shape[2])


def conv_back(cot_ext, weight):
    height = cot_ext.shape[1] - 2
    width = cot_ext.shape[2] - 2
    channels = cot_ext.shape[3]
    running = jnp.zeros((cot_ext.shape[0] * height * width, weight.shape[0]), jnp.float32)
    for row_off in range(3):
        for col_off in range(3):
            window = cot_ext[:, 2 - row_off:2 - row_off + height, 2 - col_off:2 - col_off + width, :].reshape(-1, channels)
            running = running + lax.dot_general(window, weight[:, 3 * row_off + col_off, :], (((1,), (1,)), ((), ())), preferred_element_type=jnp.float32)
    return running.reshape(cot_ext.shape[0], height, width, weight.shape[0])


def weight_terms(extended, cotangent):
    height = cotangent.shape[1]
    width = cotangent.shape[2]
    channels = extended.shape[3]
    cot_flat = cotangent.reshape(-1, cotangent.shape[3])
    listing = []
    for row_off in range(3):
        for col_off in range(3):
            window = extended[:, row_off:row_off + height, col_off:col_off + width, :].reshape(-1, channels)
            listing.append(lax.dot_general(window, cot_flat, (((0,), (0,)), ((), ())), preferred_element_type=jnp.float32))
    return jnp.stack(listing, axis=1)


def forward_segment(first_in, second_in, weight):
    branch = conv_forward(jnp.maximum(extended_of(second_in), 0), weight)
    return second_in, (first_in.astype(jnp.float32) + branch).astype(jnp.bfloat16)


def backward_segment(out_first, out_second, cot_first, cot_second, weight):
    ext_rec = jnp.maximum(extended_of(out_first), 0)
    rebuilt = (out_second.astype(jnp.float32) - conv_forward(ext_rec, weight)).astype(jnp.bfloat16)
    through = conv_back(extended_of(cot_second), weight)
    cot_rebuilt = (cot_first.astype(jnp.float32) + jnp.where(out_first > 0, through, 0.0)).astype(jnp.bfloat16)
    return (rebuilt, out_first, cot_second, cot_rebuilt), weight_terms(ext_rec, cot_second)


def reference(fwd_in, bwd_in, fresh, top_cot, conv_weight):
    scale = (2.0 * PIXELS) ** -0.5
    first_pairs = []
    first_msgs = []
    first_grads = []
    for segment_pos in range(SEGMENTS):
        weight = conv_weight[segment_pos]
        first_pairs.append(forward_segment(to_images(fwd_in[0, segment_pos]), to_images(fwd_in[1, segment_pos]), weight))
        message, grad_term = backward_segment(to_images(bwd_in[0, segment_pos]), to_images(bwd_in[1, segment_pos]), to_images(bwd_in[2, segment_pos]), to_images(bwd_in[3, segment_pos]), weight)
        first_msgs.append(message)
        first_grads.append(grad_term)
    second_pairs = []
    second_msgs = []
    grads = []
    for segment_pos in range(SEGMENTS):
        weight = conv_weight[segment_pos]
        if segment_pos == 0:
            pair_in = (to_images(fresh[0]), to_images(fresh[1]))
        else:
            pair_in = first_pairs[segment_pos - 1]
        if segment_pos == SEGMENTS - 1:
            four_in = (first_pairs[segment_pos][0], first_pairs[segment_pos][1], to_images(top_cot[0]), to_images(top_cot[1]))
        else:
            four_in = first_msgs[segment_pos + 1]
        second_pairs.append(forward_segment(pair_in[0], pair_in[1], weight))
        message, grad_term = backward_segment(four_in[0], four_in[1], four_in[2], four_in[3], weight)
        second_msgs.append(message)
        grads.append((first_grads[segment_pos] + grad_term) * scale)
    fwd_out = jnp.stack([jnp.stack([to_tiles(pair[slot]) for pair in second_pairs]) for slot in range(2)])
    bwd_out = jnp.stack([jnp.stack([to_tiles(message[slot]) for message in second_msgs]) for slot in range(4)])
    return fwd_out, bwd_out, jnp.stack(grads)
```

```python
import functools
import math

import jax
import jax.numpy as jnp
from jax import lax
from jax.experimental import pallas as pl
from jax.experimental.pallas import tpu as pltpu
from jax.sharding import PartitionSpec as P

F32 = jnp.float32
BF16 = jnp.bfloat16
TAPS = 9
TAP_ROWS = 16


class Sems:
    def __init__(self):
        self.count = 0

    def take(self, amount=1):
        first = self.count
        self.count += amount
        return first


def offsets_of(n):
    return sorted(range(1, n), key=lambda i: -min(i, n - i))


def plan(n):
    send, recv, local = Sems(), Sems(), Sems()
    numbers = {}
    for name in ("a2", "y1", "g2", "p2", "yy1", "gc2", "r"):
        numbers["halo_" + name] = (send.take(), recv.take())
    for name in ("p1", "p2", "p2h", "y1", "y1h", "y2", "gc1", "gc2", "gc2h", "fin"):
        numbers["x_" + name] = (send.take(), recv.take())
    for name in ("gather_a", "gather_b", "share", "s1_ring1", "s1_ring2", "s2_ring1", "s2_ring2"):
        numbers[name] = (send.take(n), recv.take(n))
    for name in ("s1_pair", "s2_pair"):
        numbers[name] = (send.take(), recv.take())
    for name in ("w", "y1", "g2", "a2", "a1", "y2", "g1", "fresh0", "fresh1", "top0", "top1", "last1", "o0", "o1", "o2", "o3", "o4", "o5"):
        numbers["local_" + name] = local.take()
    return numbers, send.count, recv.count, local.count


def kernel(
    n, segments, height, width, channels, scale,
    fwd, bwd, fresh, top, w,
    fwd_out, bwd_out, grad_out,
    tf, tb, pp, yy, gc, halo, n2, r1, dx1, out_a, out_b, out_c,
    s_y, s_g, s_a, s_r, s_p, s_y2, s_g2,
    wa, wr, pm, pmt, q1, q2,
    g_1, g_2, pair_send, pair_recv, sum_send, ring1, fold, ring2_send, ring2, res2, fin,
    send, recv, local,
):
    numbers = plan(n)[0]
    pixels = height * width
    half = channels // 2
    block = 2 * n
    seg = lax.axis_index("segment")
    dp = lax.axis_index("dp")
    core = dp % 2
    chip = dp // 2
    py = chip // n
    pz = chip % n
    first = jnp.where(core == 0, py, pz)
    second = jnp.where(core == 0, pz, py)
    last = segments - 1

    def at(f, g):
        y = jnp.where(core == 0, f, g)
        z = jnp.where(core == 0, g, f)
        return (seg, (y * n + z) * 2 + core)

    partner = (seg, dp + 1 - 2 * core)

    def remote(name, src, dst, device, send_slot=0, recv_slot=0):
        s, r = numbers[name]
        return pltpu.make_async_remote_copy(
            src_ref=src,
            dst_ref=dst,
            send_sem=send.at[s + send_slot],
            recv_sem=recv.at[r + recv_slot],
            device_id=device,
            device_id_type=pl.DeviceIdType.MESH,
        )

    def copy(name, src, dst):
        return pltpu.make_async_copy(src, dst, local.at[numbers["local_" + name]])

    def when(flag):
        return pl.when(flag)

    has_next = seg < last
    has_prev = seg > 0
    is_first = seg == 0
    is_last = seg == last

    load_w = copy("w", w, wa.at[second])
    load_y1 = copy("y1", bwd.at[0], tb.at[0])
    load_g2 = copy("g2", bwd.at[3], tb.at[3])
    load_a2 = copy("a2", fwd.at[1], tf.at[1])
    load_a1 = copy("a1", fwd.at[0], tf.at[0])
    load_y2 = copy("y2", bwd.at[1], tb.at[1])
    load_g1 = copy("g1", bwd.at[2], tb.at[2])
    load_fresh = [copy("fresh0", fresh.at[0], pp.at[0]), copy("fresh1", fresh.at[1], pp.at[1])]
    load_top = [
        copy("top0", top.at[0], gc.at[0]),
        copy("top1", top.at[1], gc.at[1]),
        copy("last1", fwd.at[1], yy.at[0]),
    ]

    barrier = pltpu.get_barrier_semaphore()

    def greet(device):
        pl.semaphore_signal(barrier, inc=1, device_id=device, device_id_type=pl.DeviceIdType.MESH)

    for i in offsets_of(n):
        greet(at((first + i) % n, second))
        greet(at(first, (second + i) % n))
    greet(partner)

    @when(has_next)
    def _():
        greet((seg + 1, dp))
        greet((seg + 1, partner[1]))

    @when(has_prev)
    def _():
        greet((seg - 1, dp))
        greet((seg - 1, partner[1]))

    for c in (load_w, load_y1, load_g2, load_a2, load_a1, load_y2, load_g1):
        c.start()

    @when(is_first)
    def _():
        for c in load_fresh:
            c.start()

    @when(is_last)
    def _():
        for c in load_top:
            c.start()

    def natural(k):
        c, f, g, kk = k // half, (k // block) % n, (k // 2) % n, k % 2
        even = f * (4 * n) + g * 4 + kk
        odd = g * (4 * n) + f * 4 + 2 + kk
        return jnp.where(c == 0, even, odd)

    def one_hot(flag):
        return jnp.where(flag, 1.0, 0.0).astype(BF16)

    shape = (channels, channels)
    rows = lax.broadcasted_iota(jnp.int32, shape, 0)
    cols = lax.broadcasted_iota(jnp.int32, shape, 1)
    pm[...] = one_hot(rows == natural(cols))
    pmt[...] = one_hot(natural(rows) == cols)
    shape = (block * TAP_ROWS, block * TAP_ROWS)
    rows = lax.broadcasted_iota(jnp.int32, shape, 0)
    cols = lax.broadcasted_iota(jnp.int32, shape, 1)
    q1[...] = one_hot((rows // block == cols % TAP_ROWS) & (rows % block == cols // TAP_ROWS))
    q2[...] = one_hot((cols // block == rows % TAP_ROWS) & (cols % block == rows // TAP_ROWS))
    fold[...] = jnp.zeros_like(fold)

    def matmul(a, b):
        return jnp.dot(a, b, preferred_element_type=F32)

    def build(dest, tile, edge, permute, relu):
        received = edge[...].astype(F32)
        above = jnp.where(core == 1, received, 0.0).astype(BF16)
        below = jnp.where(core == 0, received, 0.0).astype(BF16)
        whole = jnp.concatenate([above, tile[...].reshape(pixels, channels), below], axis=0)
        value = matmul(whole, pm[...]) if permute else whole.astype(F32)
        if relu:
            value = jnp.maximum(value, 0.0)
        total = pixels + 2 * width
        column = lax.broadcasted_iota(jnp.int32, (total, 1), 0) % width
        full = (height + 2, width, channels)
        dest[1] = value.astype(BF16).reshape(full)
        dest[0] = jnp.where(column == 0, 0.0, pltpu.roll(value, 1, 0)).astype(BF16).reshape(full)
        dest[2] = (
            jnp.where(column == width - 1, 0.0, pltpu.roll(value, total - 1, 0)).astype(BF16).reshape(full)
        )

    def window(s, row_off, col_off):
        return s[col_off, row_off : row_off + height].reshape(pixels, channels)

    def conv(s):
        total = None
        for t in range(TAPS):
            term = matmul(window(s, t // 3, t % 3), wr[t])
            total = term if total is None else total + term
        return total

    def conv_back(s):
        total = None
        for t in range(TAPS):
            term = lax.dot_general(
                window(s, 2 - t // 3, 2 - t % 3), wr[t], (((1,), (1,)), ((), ())), preferred_element_type=F32
            )
            total = term if total is None else total + term
        return total

    def weight_terms(dest, s, cotangent, add):
        flat = cotangent[...].reshape(pixels, channels)
        for t in range(TAPS):
            term = lax.dot_general(
                window(s, t // 3, t % 3), flat, (((0,), (0,)), ((), ())), preferred_element_type=F32
            )
            dest[t] = dest[t] + term if add else term

    def flat32(tile):
        return tile[...].reshape(pixels, channels).astype(F32)

    def as_tile(value):
        return value.astype(BF16).reshape(height, width, channels)

    def cot_rebuilt(cot_first, s_kept, s_cot):
        moved = matmul(cot_first[...].reshape(pixels, channels), pm[...])
        kept = s_kept[1, 1 : 1 + height].reshape(pixels, channels).astype(F32)
        total = moved + jnp.where(kept > 0, conv_back(s_cot), 0.0)
        return as_tile(matmul(total.astype(BF16), pmt[...]))

    load_w.wait()
    load_y1.wait()
    load_g2.wait()
    load_a2.wait()
    neighbours = 2 * (n - 1) + 1 + 2 * has_next.astype(jnp.int32) + 2 * has_prev.astype(jnp.int32)
    pl.semaphore_wait(barrier, neighbours)

    gather_a = [
        remote("gather_a", wa.at[second], wa.at[second], at(first, (second + i) % n), i, second)
        for i in offsets_of(n)
    ]
    for c in gather_a:
        c.start()

    edge_row = jnp.where(core == 0, height - 1, 0)
    halos = [
        remote("halo_y1", tb.at[0, edge_row], halo.at[1], partner),
        remote("halo_g2", tb.at[3, edge_row], halo.at[2], partner),
        remote("halo_a2", tf.at[1, edge_row], halo.at[0], partner),
    ]
    for c in halos:
        c.start()
    halo_fresh = remote("halo_p2", pp.at[1, edge_row], halo.at[3], partner)
    halo_top = [
        remote("halo_yy1", tf.at[1, edge_row], halo.at[4], partner),
        remote("halo_gc2", gc.at[1, edge_row], halo.at[5], partner),
    ]

    ahead = (seg + 1, dp)
    ahead_partner = (seg + 1, partner[1])
    behind = (seg - 1, dp)
    behind_partner = (seg - 1, partner[1])
    x_p1 = remote("x_p1", tf.at[1], pp.at[0], ahead)
    x_p2 = remote("x_p2", n2, pp.at[1], ahead)
    x_p2h = remote("x_p2h", n2.at[edge_row], halo.at[3], ahead_partner)
    x_y2 = remote("x_y2", tb.at[0], yy.at[1], behind)
    x_gc1 = remote("x_gc1", tb.at[3], gc.at[0], behind)
    x_y1 = remote("x_y1", r1, yy.at[0], behind)
    x_y1h = remote("x_y1h", r1.at[edge_row], halo.at[4], behind_partner)
    x_gc2 = remote("x_gc2", dx1, gc.at[1], behind)
    x_gc2h = remote("x_gc2h", dx1.at[edge_row], halo.at[5], behind_partner)
    x_fin = remote("x_fin", res2, fin, behind)

    @when(has_prev)
    def _():
        x_y2.start()
        x_gc1.start()

    @when(has_next)
    def _():
        x_p1.start()

    @when(is_first)
    def _():
        for c in load_fresh:
            c.wait()
        halo_fresh.start()

    @when(is_last)
    def _():
        for c in load_top:
            c.wait()
        for c in halo_top:
            c.start()

    other_half = pl.multiple_of((1 - core) * half, half)
    own_half = pl.multiple_of(core * half, half)
    own_block = pl.multiple_of(first * block, block)

    def scatter(k, g):
        tag = f"s{k + 1}_"
        pair = remote(tag + "pair", pair_send.at[k], pair_recv.at[k], partner)
        sends1 = []
        for i in offsets_of(n):
            peer = (first + i) % n
            rows = pl.ds(pl.multiple_of(peer * block, block), block)
            sends1.append(
                remote(tag + "ring1", sum_send.at[k, :, rows], ring1.at[k, first], at(peer, second), i, first)
            )
        sends2 = []
        for i in offsets_of(n):
            peer = (second + i) % n
            sends2.append(
                remote(tag + "ring2", ring2_send.at[k, peer], ring2.at[k, second], at(first, peer), i, second)
            )

        def stage0():
            pair_send[k] = g[:, pl.ds(other_half, half), :].astype(BF16)
            pair.start()

        def stage1_sum():
            pair.wait_recv()
            sum_send[k] = (g[:, pl.ds(own_half, half), :] + pair_recv[k].astype(F32)).astype(BF16)

        def stage1_send():
            for c in sends1:
                c.start()

        def stage2():
            total = sum_send[k, :, pl.ds(own_block, block), :].astype(F32)
            for i in reversed(offsets_of(n)):
                peer = (first + n - i) % n
                remote(tag + "ring1", ring1.at[k, peer], ring1.at[k, peer], partner, i, peer).wait_recv()
                total = total + ring1[k, peer].astype(F32)
            fold[0:TAPS] = total.astype(BF16)
            sorted_rows = matmul(q2[...], fold[...].reshape(TAP_ROWS * block, channels))
            ring2_send[k] = sorted_rows.astype(BF16).reshape(n, 2, TAP_ROWS, channels)
            for c in sends2:
                c.start()

        def stage3():
            total = ring2_send[k, second].astype(F32)
            for i in reversed(offsets_of(n)):
                peer = (second + n - i) % n
                remote(tag + "ring2", ring2.at[k, peer], ring2.at[k, peer], partner, i, peer).wait_recv()
                total = total + ring2[k, peer].astype(F32)
            return total

        def finish():
            pair.wait_send()
            for c in sends1 + sends2:
                c.wait_send()

        return stage0, stage1_sum, stage1_send, stage2, stage3, finish

    one = scatter(0, g_1)
    two = scatter(1, g_2)

    halos[0].wait_recv()
    build(s_y, tb.at[0], halo.at[1], True, True)
    halos[1].wait_recv()
    build(s_g, tb.at[3], halo.at[2], False, False)

    for i in reversed(offsets_of(n)):
        peer = (second + n - i) % n
        remote("gather_a", wa.at[peer], wa.at[peer], partner, i, peer).wait_recv()
    line = matmul(q1[...], wa[...].reshape(block * TAP_ROWS, channels)).astype(BF16)
    mine = pl.multiple_of(own_half + own_block, block)
    wr[:, pl.ds(mine, block), :] = line[: TAPS * block].reshape(TAPS, block, channels)

    def share(f):
        rows = pl.ds(pl.multiple_of(own_half + f * block, block), block)
        return remote("share", wr.at[:, rows], wr.at[:, rows], partner, f, f)

    mine_rows = pl.ds(mine, block)
    gather_b = [
        remote("gather_b", wr.at[:, mine_rows], wr.at[:, mine_rows], at((first + i) % n, second), i, first)
        for i in offsets_of(n)
    ]
    for c in gather_b:
        c.start()
    share(first).start()

    weight_terms(g_1, s_y, tb.at[3], False)
    halos[2].wait_recv()
    build(s_a, tf.at[1], halo.at[0], True, True)

    @when(is_last)
    def _():
        weight_terms(g_1, s_a, gc.at[1], True)

    one[0]()

    for i in reversed(offsets_of(n)):
        peer = (first + n - i) % n
        rows = pl.ds(pl.multiple_of(own_half + peer * block, block), block)
        remote("gather_b", wr.at[:, rows], wr.at[:, rows], partner, i, peer).wait_recv()
        share(peer).start()
    one[1]()
    for f in range(n):
        rows = pl.ds(pl.multiple_of(other_half + f * block, block), block)
        remote("share", wr.at[:, rows], wr.at[:, rows], partner, f, f).wait_recv()
    one[2]()

    load_y2.wait()
    r1[...] = as_tile(flat32(tb.at[1]) - conv(s_y))
    halo_r = remote("halo_r", r1.at[edge_row], halo.at[6], partner)

    @when(has_prev)
    def _():
        halo_r.start()
        x_y1h.start()
        x_y1.start()

    load_g1.wait()
    dx1[...] = cot_rebuilt(tb.at[2], s_y, s_g)

    @when(has_prev)
    def _():
        x_gc2h.start()
        x_gc2.start()
        halo_r.wait_recv()
        build(s_r, r1, halo.at[6], True, True)
        weight_terms(g_2, s_r, dx1, False)
        two[0]()

    load_a1.wait()
    n2[...] = as_tile(flat32(tf.at[0]) + conv(s_a))

    @when(has_next)
    def _():
        x_p2h.start()
        x_p2.start()

    @when(is_last)
    def _():
        yy[1] = n2[...]

    @when(has_prev)
    def _():
        two[1]()
        two[2]()

    def ready(local_flag, names):
        @when(jnp.logical_not(local_flag))
        def _():
            for name, ref in names:
                remote(name, ref, ref, partner).wait_recv()

    @when(is_last)
    def _():
        for c in halo_top:
            c.wait_recv()

    @when(is_first)
    def _():
        halo_fresh.wait_recv()

    ready(is_last, [("x_y1h", halo.at[4]), ("x_y1", yy.at[0]), ("x_y2", yy.at[1])])
    build(s_y2, yy.at[0], halo.at[4], True, True)
    out_b[...] = as_tile(flat32(yy.at[1]) - conv(s_y2))
    out = [copy("o0", out_b, bwd_out.at[0]), copy("o1", yy.at[0], bwd_out.at[1])]

    one[3]()

    ready(is_first, [("x_p2h", halo.at[3]), ("x_p2", pp.at[1]), ("x_p1", pp.at[0])])
    build(s_p, pp.at[1], halo.at[3], True, True)
    out_a[...] = as_tile(flat32(pp.at[0]) + conv(s_p))
    out += [copy("o2", pp.at[1], fwd_out.at[0]), copy("o3", out_a, fwd_out.at[1])]
    for c in out:
        c.start()

    @when(has_prev)
    def _():
        two[3]()

    ready(is_last, [("x_gc2h", halo.at[5]), ("x_gc2", gc.at[1]), ("x_gc1", gc.at[0])])
    build(s_g2, gc.at[1], halo.at[5], False, False)
    out_c[...] = cot_rebuilt(gc.at[0], s_y2, s_g2)
    more = [copy("o4", gc.at[1], bwd_out.at[2]), copy("o5", out_c, bwd_out.at[3])]
    for c in more:
        c.start()
    total = one[4]()
    grad_out[...] = total

    @when(has_prev)
    def _():
        res2[...] = two[4]()
        x_fin.start()

    @when(has_next)
    def _():
        x_fin.wait_recv()
        grad_out[...] = grad_out[...] + fin[...]

    grad_out[...] = grad_out[...] * scale

    for c in gather_a + gather_b + halos:
        c.wait_send()
    for f in range(n):
        share(f).wait_send()
    one[5]()

    @when(has_prev)
    def _():
        for c in (x_y2, x_gc1, x_y1, x_y1h, x_gc2, x_gc2h, x_fin, halo_r):
            c.wait_send()
        two[5]()

    @when(has_next)
    def _():
        for c in (x_p1, x_p2, x_p2h):
            c.wait_send()

    @when(is_first)
    def _():
        halo_fresh.wait_send()

    @when(is_last)
    def _():
        for c in halo_top:
            c.wait_send()

    for c in out + more:
        c.wait()


def fused(n, segments, scale, fwd, bwd, fresh, top, w):
    height, width, channels = fwd.shape[1:]
    tile = (height, width, channels)
    shifted = (3, height + 2, width, channels)
    half = channels // 2
    block = 2 * n
    _, n_send, n_recv, n_local = plan(n)
    square = (channels, channels)
    mixed = (block * TAP_ROWS, block * TAP_ROWS)
    v = pltpu.VMEM
    scratch = [
        v((2, *tile), BF16),
        v((4, *tile), BF16),
        v((2, *tile), BF16),
        v((2, *tile), BF16),
        v((2, *tile), BF16),
        v((7, width, channels), BF16),
        v(tile, BF16),
        v(tile, BF16),
        v(tile, BF16),
        v(tile, BF16),
        v(tile, BF16),
        v(tile, BF16),
        *[v(shifted, BF16)] * 7,
        v((n, 2, TAP_ROWS, channels), BF16),
        v((TAPS, channels, channels), BF16),
        v(square, BF16),
        v(square, BF16),
        v(mixed, BF16),
        v(mixed, BF16),
        v((TAPS, channels, channels), F32),
        v((TAPS, channels, channels), F32),
        v((2, TAPS, half, channels), BF16),
        v((2, TAPS, half, channels), BF16),
        v((2, TAPS, half, channels), BF16),
        v((2, n, TAPS, block, channels), BF16),
        v((TAP_ROWS, block, channels), BF16),
        v((2, n, 2, TAP_ROWS, channels), BF16),
        v((2, n, 2, TAP_ROWS, channels), BF16),
        v((2, TAP_ROWS, channels), F32),
        v((2, TAP_ROWS, channels), F32),
        pltpu.SemaphoreType.DMA((n_send,)),
        pltpu.SemaphoreType.DMA((n_recv,)),
        pltpu.SemaphoreType.DMA((n_local,)),
    ]
    return pl.pallas_call(
        functools.partial(kernel, n, segments, height, width, channels, scale),
        out_shape=(
            jax.ShapeDtypeStruct((2, *tile), BF16),
            jax.ShapeDtypeStruct((4, *tile), BF16),
            jax.ShapeDtypeStruct((2, TAP_ROWS, channels), F32),
        ),
        in_specs=[pl.BlockSpec(memory_space=pl.ANY)] * 5,
        out_specs=(
            pl.BlockSpec(memory_space=pl.ANY),
            pl.BlockSpec(memory_space=pl.ANY),
            pl.BlockSpec(memory_space=pltpu.VMEM),
        ),
        scratch_shapes=scratch,
        compiler_params=pltpu.CompilerParams(collective_id=0, has_side_effects=True),
        name="coupling",
    )(fwd, bwd, fresh, top, w)


def shards(segments, tiles, fwd_in, bwd_in, fresh, top_cot, conv_weight):
    height, width, channels = fwd_in.shape[3:]
    n = math.isqrt(tiles // 2)
    scale = (2.0 * tiles * height * width) ** (-0.5)
    weight = jnp.pad(conv_weight[0], ((0, 0), (0, TAP_ROWS - TAPS), (0, 0)))
    forward, message, grad = fused(
        n, segments, scale, fwd_in[:, 0, 0], bwd_in[:, 0, 0], fresh[:, 0], top_cot[:, 0], weight
    )
    return forward[:, None, None], message[:, None, None], grad[None, :, :TAPS]


def solution(mesh):
    segments = mesh.shape["segment"]
    tiles = mesh.shape["dp"]
    streams = P(None, "segment", "dp", None, None, None)
    halves = P(None, "dp", None, None, None)
    weights = P("segment", "dp", None, None)
    return jax.shard_map(
        functools.partial(shards, segments, tiles),
        mesh=mesh,
        in_specs=(streams, streams, halves, halves, weights),
        out_specs=(streams, streams, weights),
        check_vma=False,
    )
```

```python
import functools
import math

import jax
import jax.numpy as jnp
from jax import lax
from jax.experimental import pallas as pl
from jax.experimental.pallas import tpu as pltpu
from jax.sharding import PartitionSpec as P

F32 = jnp.float32
BF16 = jnp.bfloat16
TAPS = 9
TAP_ROWS = 16
GROUPS = (((0, 9),), ((0, 3), (3, 6), (6, 9)))
SPLIT = 5


class Sems:
    def __init__(self):
        self.count = 0

    def take(self, amount=1):
        first = self.count
        self.count += amount
        return first


def offsets_of(n):
    return sorted(range(1, n), key=lambda i: -min(i, n - i))


def plan(n):
    send, recv, local = Sems(), Sems(), Sems()
    sends = ("gather_a", "gather_b", "share", "halo", "edge", "x_back", "x_back_row", "x_ahead", "x_ahead_row", "x_fin")
    sends = {name: send.take() for name in sends + ("s1_ring1", "s2_ring1", "s1_ring2", "s2_ring2")}
    recvs = ("gather_a", "share", "h_yg", "h_a2", "h_r", "h_p", "h_y", "h_g", "x_pp", "x_yy", "x_gc", "x_fin")
    recvs = {name: recv.take() for name in recvs + ("s1_ring1", "s2_ring1", "s1_ring2", "s2_ring2", "s1_relay", "s2_relay")}
    recvs["gather_b"] = recv.take(n)
    for name, parts in (("s1_pair", len(GROUPS[0])), ("s2_pair", len(GROUPS[1]))):
        sends[name] = send.take()
        recvs[name] = recv.take(parts)
    locals_ = {name: local.take() for name in ("w", "y1", "g2", "a2", "a1", "mid", "fresh", "top", "last1", "fo", "bo")}
    return sends, recvs, locals_, send.count, recv.count, local.count


def kernel(
    n, segments, height, width, channels, scale,
    fwd, bwd, fresh, top, w,
    fwd_out, bwd_out, grad_out,
    tf, tb, pp, yy, gc, halo, n2, r1, dx1, out_a, out_b, out_c,
    s_y, s_g, s_a, s_r, s_p, s_y2, s_g2,
    wa, wr, pm, pmt, q2, rows_f32,
    g_1, g_2, pair_send, pair_recv, sum_send, relayed, ring1, fold, ring2_send, ring2, res2, fin,
    send, recv, local,
):
    sends, recvs, locals_ = plan(n)[:3]
    far = n // 2 - 1
    pixels = height * width
    half = channels // 2
    block = 2 * n
    seg = lax.axis_index("segment")
    dp = lax.axis_index("dp")
    core = dp % 2
    chip = dp // 2
    py = chip // n
    pz = chip % n
    first = jnp.where(core == 0, py, pz)
    second = jnp.where(core == 0, pz, py)
    last = segments - 1

    def at(f, g):
        y = jnp.where(core == 0, f, g)
        z = jnp.where(core == 0, g, f)
        return (seg, (y * n + z) * 2 + core)

    partner = (seg, dp + 1 - 2 * core)

    def remote(send_name, recv_name, src, dst, device, recv_slot=0):
        return pltpu.make_async_remote_copy(
            src_ref=src,
            dst_ref=dst,
            send_sem=send.at[sends[send_name]],
            recv_sem=recv.at[recvs[recv_name] + recv_slot],
            device_id=device,
            device_id_type=pl.DeviceIdType.MESH,
        )

    def arrived(recv_name, ref, recv_slot=0):
        remote("halo", recv_name, ref, ref, partner, recv_slot).wait_recv()

    def sent(send_name, ref):
        remote(send_name, "share", ref, ref, partner).wait_send()

    def copy(name, src, dst):
        return pltpu.make_async_copy(src, dst, local.at[locals_[name]])

    def when(flag):
        return pl.when(flag)

    has_next = seg < last
    has_prev = seg > 0
    is_first = seg == 0
    is_last = seg == last

    load_w = copy("w", w, wa.at[second])
    load_y1 = copy("y1", bwd.at[0], tb.at[0])
    load_g2 = copy("g2", bwd.at[3], tb.at[3])
    load_a2 = copy("a2", fwd.at[1], tf.at[1])
    load_a1 = copy("a1", fwd.at[0], tf.at[0])
    load_mid = copy("mid", bwd.at[1:3], tb.at[1:3])
    load_fresh = copy("fresh", fresh, pp)
    load_top = copy("top", top, gc)
    load_last = copy("last1", fwd.at[1], yy.at[0])

    barrier = pltpu.get_barrier_semaphore()

    def greet(device):
        pl.semaphore_signal(barrier, inc=1, device_id=device, device_id_type=pl.DeviceIdType.MESH)

    for i in offsets_of(n):
        greet(at((first + i) % n, second))
        greet(at(first, (second + i) % n))
    greet(partner)

    @when(has_next)
    def _():
        greet((seg + 1, dp))
        greet((seg + 1, partner[1]))

    @when(has_prev)
    def _():
        greet((seg - 1, dp))
        greet((seg - 1, partner[1]))

    for c in (load_w, load_y1, load_g2, load_a2, load_a1, load_mid):
        c.start()

    @when(is_first)
    def _():
        load_fresh.start()

    @when(is_last)
    def _():
        load_top.start()
        load_last.start()

    def natural(k):
        c, f, g, kk = k // half, (k // block) % n, (k // 2) % n, k % 2
        even = f * (4 * n) + g * 4 + kk
        odd = g * (4 * n) + f * 4 + 2 + kk
        return jnp.where(c == 0, even, odd)

    def one_hot(flag):
        return jnp.where(flag, 1.0, 0.0).astype(BF16)

    shape = (channels, channels)
    rows = lax.broadcasted_iota(jnp.int32, shape, 0)
    cols = lax.broadcasted_iota(jnp.int32, shape, 1)
    pm[...] = one_hot(rows == natural(cols))
    pmt[...] = one_hot(natural(rows) == cols)
    shape = (block * TAP_ROWS, block * TAP_ROWS)
    rows = lax.broadcasted_iota(jnp.int32, shape, 0)
    cols = lax.broadcasted_iota(jnp.int32, shape, 1)
    q2[...] = one_hot(
        (rows // (2 * TAP_ROWS) == (cols % block) // 2)
        & ((rows // 2) % TAP_ROWS == cols // block)
        & (rows % 2 == cols % 2)
    )
    fold[...] = jnp.zeros_like(fold)

    def matmul(a, b):
        return jnp.dot(a, b, preferred_element_type=F32)

    def build(dest, tile, edge, permute, relu):
        received = edge[...].astype(F32)
        above = jnp.where(core == 1, received, 0.0).astype(BF16)
        below = jnp.where(core == 0, received, 0.0).astype(BF16)
        whole = jnp.concatenate([above, tile[...].reshape(pixels, channels), below], axis=0)
        value = matmul(whole, pm[...]) if permute else whole.astype(F32)
        if relu:
            value = jnp.maximum(value, 0.0)
        total = pixels + 2 * width
        column = lax.broadcasted_iota(jnp.int32, (total, 1), 0) % width
        full = (height + 2, width, channels)
        dest[1] = value.astype(BF16).reshape(full)
        dest[0] = jnp.where(column == 0, 0.0, pltpu.roll(value, 1, 0)).astype(BF16).reshape(full)
        dest[2] = (
            jnp.where(column == width - 1, 0.0, pltpu.roll(value, total - 1, 0)).astype(BF16).reshape(full)
        )

    def window(s, row_off, col_off):
        return s[col_off, row_off : row_off + height].reshape(pixels, channels)

    def conv(s):
        total = None
        for t in range(TAPS):
            term = matmul(window(s, t // 3, t % 3), wr[t])
            total = term if total is None else total + term
        return total

    def conv_back(s):
        total = None
        for t in range(TAPS):
            term = lax.dot_general(
                window(s, 2 - t // 3, 2 - t % 3), wr[t], (((1,), (1,)), ((), ())), preferred_element_type=F32
            )
            total = term if total is None else total + term
        return total

    def weight_terms(dest, s, cotangent, add, t):
        flat = cotangent[...].reshape(pixels, channels)
        term = lax.dot_general(
            window(s, t // 3, t % 3), flat, (((0,), (0,)), ((), ())), preferred_element_type=F32
        )
        dest[t] = dest[t] + term if add else term

    def flat32(tile):
        return tile[...].reshape(pixels, channels).astype(F32)

    def as_tile(value):
        return value.astype(BF16).reshape(height, width, channels)

    def cot_rebuilt(cot_first, s_kept, s_cot):
        moved = matmul(cot_first[...].reshape(pixels, channels), pm[...])
        kept = s_kept[1, 1 : 1 + height].reshape(pixels, channels).astype(F32)
        total = moved + jnp.where(kept > 0, conv_back(s_cot), 0.0)
        return as_tile(matmul(total.astype(BF16), pmt[...]))

    load_w.wait()
    load_y1.wait()
    load_g2.wait()
    load_a2.wait()
    neighbours = 2 * (n - 1) + 1 + 2 * has_next.astype(jnp.int32) + 2 * has_prev.astype(jnp.int32)
    pl.semaphore_wait(barrier, neighbours)

    for i in offsets_of(n):
        remote("gather_a", "gather_a", wa.at[second], wa.at[second], at(first, (second + i) % n)).start()

    edge_row = jnp.where(core == 0, height - 1, 0)
    remote("halo", "h_yg", tb.at[0, edge_row], halo.at[1], partner).start()
    remote("halo", "h_yg", tb.at[3, edge_row], halo.at[2], partner).start()
    remote("halo", "h_a2", tf.at[1, edge_row], halo.at[0], partner).start()

    ahead = (seg + 1, dp)
    ahead_partner = (seg + 1, partner[1])
    behind = (seg - 1, dp)
    behind_partner = (seg - 1, partner[1])

    @when(has_prev)
    def _():
        remote("x_back", "x_yy", tb.at[0], yy.at[1], behind).start()
        remote("x_back", "x_gc", tb.at[3], gc.at[0], behind).start()

    @when(has_next)
    def _():
        remote("x_ahead", "x_pp", tf.at[1], pp.at[0], ahead).start()

    @when(is_first)
    def _():
        load_fresh.wait()
        remote("edge", "h_p", pp.at[1, edge_row], halo.at[3], partner).start()

    @when(is_last)
    def _():
        load_top.wait()
        load_last.wait()
        remote("edge", "h_y", tf.at[1, edge_row], halo.at[4], partner).start()
        remote("edge", "h_g", gc.at[1, edge_row], halo.at[5], partner).start()

    other_half = pl.multiple_of((1 - core) * half, half)
    own_half = pl.multiple_of(core * half, half)
    own_block = pl.multiple_of(first * block, block)

    def block_rows(f):
        return pl.ds(pl.multiple_of(f * block, block), block)

    def scatter(k, g):
        tag = f"s{k + 1}_"
        relay_taps = ((slice(0, SPLIT), 1), (slice(SPLIT, TAPS), -1))

        def pair_start(part):
            lo, hi = GROUPS[k][part]
            pair_send[k, lo:hi] = g[lo:hi, pl.ds(other_half, half), :].astype(BF16)
            src, dst = pair_send.at[k, lo:hi], pair_recv.at[k, lo:hi]
            remote(tag + "pair", tag + "pair", src, dst, partner, part).start()

        def pair_sum():
            for part, (lo, hi) in enumerate(GROUPS[k]):
                arrived(tag + "pair", pair_recv.at[k, lo:hi], part)
                own = g[lo:hi, pl.ds(own_half, half), :]
                sum_send[k, lo:hi] = (own + pair_recv[k, lo:hi].astype(F32)).astype(BF16)

        def ring_send(i):
            peer = (first + n + i) % n
            src = sum_send.at[k, :, block_rows(peer)]
            remote(tag + "ring1", tag + "ring1", src, ring1.at[k, first], at(peer, second)).start()

        def ring1_near():
            if far > 0:
                for taps, way in relay_taps:
                    src = sum_send.at[k, taps, block_rows((first + n // 2) % n)]
                    dst = relayed.at[k, taps]
                    device = at((first + n + way) % n, second)
                    remote(tag + "ring1", tag + "relay", src, dst, device).start()
                for i in range(far - 1, 0, -1):
                    ring_send(i)
                    ring_send(-i)
            else:
                ring_send(1)

        def ring1_far():
            if far > 0:
                arrived(tag + "relay", relayed.at[k])
                for taps, way in relay_taps:
                    rows = block_rows((first + n + way * far) % n)
                    own = sum_send[k, taps, rows, :].astype(F32)
                    sum_send[k, taps, rows, :] = (own + relayed[k, taps].astype(F32)).astype(BF16)
                ring_send(far)
                ring_send(-far)

        def ring2_start():
            total = sum_send[k, :, pl.ds(own_block, block), :].astype(F32)
            near = [i for i in range(1, n) if far == 0 or i != n // 2]
            arrived(tag + "ring1", ring1.at[k, 0 : len(near)])
            for i in near:
                total = total + ring1[k, (first + i) % n].astype(F32)
            fold[0:TAPS] = total.astype(BF16)
            sorted_rows = matmul(q2[...], fold[...].reshape(TAP_ROWS * block, channels))
            ring2_send[k] = sorted_rows.astype(BF16).reshape(n, 2 * TAP_ROWS, channels)
            for i in offsets_of(n):
                peer = (second + i) % n
                src, dst = ring2_send.at[k, peer], ring2.at[k, second]
                remote(tag + "ring2", tag + "ring2", src, dst, at(first, peer)).start()

        def ring2_sum():
            total = ring2_send[k, second].astype(F32)
            arrived(tag + "ring2", ring2.at[k, 0 : n - 1])
            for i in range(1, n):
                total = total + ring2[k, (second + i) % n].astype(F32)
            return total[0 : 2 * TAPS + 6]

        def finish():
            sent(tag + "pair", pair_send.at[k])
            sent(tag + "ring1", sum_send.at[k, :, 0 : (n - 1) * block])
            sent(tag + "ring2", ring2_send.at[k, 0 : n - 1])

        return pair_start, pair_sum, ring1_near, ring1_far, ring2_start, ring2_sum, finish

    one_pair, one_sum, one_near, one_far, one_ring2, one_total, one_finish = scatter(0, g_1)
    two_pair, two_sum, two_near, two_far, two_ring2, two_total, two_finish = scatter(1, g_2)

    arrived("h_yg", halo.at[1:3])
    build(s_y, tb.at[0], halo.at[1], True, True)
    build(s_g, tb.at[3], halo.at[2], False, False)

    def weight_rows(c, f):
        return pl.ds(pl.multiple_of(c * half + f * block, block), block)

    arrived("gather_a", wa.at[0 : n - 1])
    for g in range(n):
        for t in range(TAPS):
            rows_f32[t * block + 2 * g : t * block + 2 * g + 2, :] = wa[g, t].astype(F32)
    mine = weight_rows(core, first)
    wr[:, mine, :] = rows_f32[...].astype(BF16).reshape(TAPS, block, channels)

    def weight_send(src, way, taps, slot):
        ref = wr.at[taps, weight_rows(core, src)]
        remote("gather_b", "gather_b", ref, ref, at((first + n + way) % n, second), slot).start()

    def share(f):
        ref = wr.at[:, weight_rows(core, f)]
        remote("share", "share", ref, ref, partner).start()

    def weights_from(f):
        arrived("gather_b", wr.at[:, weight_rows(core, f)], f)

    every = slice(0, TAPS)
    reach = range(far, 0, -1) if far > 0 else [1]
    for i in reach:
        weight_send(first, i, every, first)
        if far > 0:
            weight_send(first, -i, every, first)
    share(first)

    for t in range(TAPS):
        weight_terms(g_1, s_y, tb.at[3], False, t)
    arrived("h_a2", halo.at[0])
    build(s_a, tf.at[1], halo.at[0], True, True)

    @when(is_last)
    def _():
        for t in range(TAPS):
            weight_terms(g_1, s_a, gc.at[1], True, t)

    one_pair(0)

    opposite = (first + n // 2) % n
    if far > 0:
        for way in (1, -1):
            origin = (first + n + way * far) % n
            weights_from(origin)
            taps = slice(0, SPLIT) if way > 0 else slice(SPLIT, TAPS)
            receiver = (first + n - way) % n
            slot = origin if way > 0 else receiver
            weight_send(origin, -way, taps, slot)
            share(origin)
        for i in range(1, far):
            for way in (1, -1):
                origin = (first + n + way * i) % n
                weights_from(origin)
                share(origin)
        arrived("gather_b", wr.at[0:SPLIT, weight_rows(core, opposite)], opposite)
        arrived("gather_b", wr.at[SPLIT:TAPS, weight_rows(core, opposite)], first)
    else:
        weights_from(opposite)
    share(opposite)
    one_sum()
    arrived("share", wr.at[:, pl.ds(other_half, half)])
    one_near()

    load_mid.wait()
    r1[...] = as_tile(flat32(tb.at[1]) - conv(s_y))

    @when(has_prev)
    def _():
        remote("x_back_row", "h_r", r1.at[edge_row], halo.at[6], partner).start()
        remote("x_back_row", "h_y", r1.at[edge_row], halo.at[4], behind_partner).start()
        remote("x_back", "x_yy", r1, yy.at[0], behind).start()

    dx1[...] = cot_rebuilt(tb.at[2], s_y, s_g)

    @when(has_prev)
    def _():
        remote("x_back_row", "h_g", dx1.at[edge_row], halo.at[5], behind_partner).start()
        remote("x_back", "x_gc", dx1, gc.at[1], behind).start()
        arrived("h_r", halo.at[6])
        build(s_r, r1, halo.at[6], True, True)
        for part, (lo, hi) in enumerate(GROUPS[1]):
            for t in range(lo, hi):
                weight_terms(g_2, s_r, dx1, False, t)
            two_pair(part)

    one_far()
    load_a1.wait()
    n2[...] = as_tile(flat32(tf.at[0]) + conv(s_a))

    @when(has_next)
    def _():
        remote("x_ahead_row", "h_p", n2.at[edge_row], halo.at[3], ahead_partner).start()
        remote("x_ahead", "x_pp", n2, pp.at[1], ahead).start()

    @when(is_last)
    def _():
        yy[1] = n2[...]

    @when(has_prev)
    def _():
        two_sum()
        two_near()
        two_far()

    arrived("h_y", halo.at[4])

    @when(has_next)
    def _():
        arrived("x_yy", yy)

    build(s_y2, yy.at[0], halo.at[4], True, True)
    out_b[...] = as_tile(flat32(yy.at[1]) - conv(s_y2))
    copy("bo", out_b, bwd_out.at[0]).start()
    copy("bo", yy.at[0], bwd_out.at[1]).start()

    one_ring2()

    arrived("h_p", halo.at[3])

    @when(has_prev)
    def _():
        arrived("x_pp", pp)

    build(s_p, pp.at[1], halo.at[3], True, True)
    out_a[...] = as_tile(flat32(pp.at[0]) + conv(s_p))
    copy("fo", pp.at[1], fwd_out.at[0]).start()
    copy("fo", out_a, fwd_out.at[1]).start()

    @when(has_prev)
    def _():
        two_ring2()

    arrived("h_g", halo.at[5])

    @when(has_next)
    def _():
        arrived("x_gc", gc)

    build(s_g2, gc.at[1], halo.at[5], False, False)
    out_c[...] = cot_rebuilt(gc.at[0], s_y2, s_g2)
    copy("bo", gc.at[1], bwd_out.at[2]).start()
    copy("bo", out_c, bwd_out.at[3]).start()
    rows_f32[0 : 2 * TAPS + 6, :] = one_total()

    @when(has_prev)
    def _():
        res2[...] = two_total()
        remote("x_fin", "x_fin", res2, fin, behind).start()

    @when(has_next)
    def _():
        arrived("x_fin", fin)
        rows_f32[0 : 2 * TAPS + 6, :] = rows_f32[0 : 2 * TAPS + 6, :] + fin[...]

    for t in range(TAPS):
        grad_out[t] = rows_f32[2 * t : 2 * t + 2, :] * scale

    sent("gather_a", wa.at[0 : n - 1])
    sent("gather_b", wr.at[:, 0 : (n - 1) * block])
    sent("share", wr.at[:, pl.ds(other_half, half)])
    sent("halo", halo.at[0:3])
    one_finish()

    @when(has_prev)
    def _():
        sent("x_back", tb)
        sent("x_back_row", halo.at[0:3])
        sent("x_fin", fin)
        two_finish()

    @when(has_next)
    def _():
        sent("x_ahead", tf)
        sent("x_ahead_row", halo.at[0])

    @when(is_first)
    def _():
        sent("edge", halo.at[0])

    @when(is_last)
    def _():
        sent("edge", halo.at[0:2])

    copy("fo", fwd_out, fwd_out).wait()
    copy("bo", bwd_out, bwd_out).wait()


def fused(n, segments, scale, fwd, bwd, fresh, top, w):
    height, width, channels = fwd.shape[1:]
    tile = (height, width, channels)
    shifted = (3, height + 2, width, channels)
    half = channels // 2
    block = 2 * n
    n_send, n_recv, n_local = plan(n)[3:]
    square = (channels, channels)
    mixed = (block * TAP_ROWS, block * TAP_ROWS)
    v = pltpu.VMEM
    scratch = [
        v((2, *tile), BF16),
        v((4, *tile), BF16),
        v((2, *tile), BF16),
        v((2, *tile), BF16),
        v((2, *tile), BF16),
        v((7, width, channels), BF16),
        v(tile, BF16),
        v(tile, BF16),
        v(tile, BF16),
        v(tile, BF16),
        v(tile, BF16),
        v(tile, BF16),
        *[v(shifted, BF16)] * 7,
        v((n, TAPS, 2, channels), BF16),
        v((TAPS, channels, channels), BF16),
        v(square, BF16),
        v(square, BF16),
        v(mixed, BF16),
        v((max(TAPS * block, 2 * TAPS + 6), channels), F32),
        v((TAPS, channels, channels), F32),
        v((TAPS, channels, channels), F32),
        v((2, TAPS, half, channels), BF16),
        v((2, TAPS, half, channels), BF16),
        v((2, TAPS, half, channels), BF16),
        v((2, TAPS, block, channels), BF16),
        v((2, n, TAPS, block, channels), BF16),
        v((TAP_ROWS, block, channels), BF16),
        v((2, n, 2 * TAP_ROWS, channels), BF16),
        v((2, n, 2 * TAP_ROWS, channels), BF16),
        v((2 * TAPS + 6, channels), F32),
        v((2 * TAPS + 6, channels), F32),
        pltpu.SemaphoreType.DMA((n_send,)),
        pltpu.SemaphoreType.DMA((n_recv,)),
        pltpu.SemaphoreType.DMA((n_local,)),
    ]
    return pl.pallas_call(
        functools.partial(kernel, n, segments, height, width, channels, scale),
        out_shape=(
            jax.ShapeDtypeStruct((2, *tile), BF16),
            jax.ShapeDtypeStruct((4, *tile), BF16),
            jax.ShapeDtypeStruct((TAPS, 2, channels), F32),
        ),
        in_specs=[pl.BlockSpec(memory_space=pltpu.HBM)] * 5,
        out_specs=(
            pl.BlockSpec(memory_space=pl.ANY),
            pl.BlockSpec(memory_space=pl.ANY),
            pl.BlockSpec(memory_space=pltpu.VMEM),
        ),
        scratch_shapes=scratch,
        compiler_params=pltpu.CompilerParams(collective_id=0, has_side_effects=True, vmem_limit_bytes=44 << 20),
        name="coupling",
    )(fwd, bwd, fresh, top, w)


def shards(segments, tiles, fwd_in, bwd_in, fresh, top_cot, conv_weight):
    height, width, channels = fwd_in.shape[3:]
    n = math.isqrt(tiles // 2)
    scale = (2.0 * tiles * height * width) ** (-0.5)
    weight = conv_weight[0].transpose(1, 0, 2)
    forward, message, grad = fused(
        n, segments, scale, fwd_in[:, 0, 0], bwd_in[:, 0, 0], fresh[:, 0], top_cot[:, 0], weight
    )
    return forward[:, None, None], message[:, None, None], grad.transpose(1, 0, 2)[None]


def solution(mesh):
    segments = mesh.shape["segment"]
    tiles = mesh.shape["dp"]
    streams = P(None, "segment", "dp", None, None, None)
    halves = P(None, "dp", None, None, None)
    weights = P("segment", "dp", None, None)
    return jax.shard_map(
        functools.partial(shards, segments, tiles),
        mesh=mesh,
        in_specs=(streams, streams, halves, halves, weights),
        out_specs=(streams, streams, weights),
        check_vma=False,
    )
```

```python
import functools
import math

import jax
import jax.numpy as jnp
from jax import lax
from jax.experimental import pallas as pl
from jax.experimental.pallas import tpu as pltpu
from jax.sharding import PartitionSpec as P

F32 = jnp.float32
BF16 = jnp.bfloat16
TAPS = 9
TAP_ROWS = 16
GROUPS = (((0, 9),), ((0, 3), (3, 6), (6, 9)))
SPLIT = 5


class Sems:
    def __init__(self):
        self.count = 0

    def take(self, amount=1):
        first = self.count
        self.count += amount
        return first


def offsets_of(n):
    return sorted(range(1, n), key=lambda i: -min(i, n - i))


def plan(n):
    send, recv, local = Sems(), Sems(), Sems()
    sends = ("gather_a", "gather_b", "share", "halo", "edge", "x_back", "x_back_row", "x_ahead", "x_ahead_row", "x_fin")
    sends = {name: send.take() for name in sends + ("s1_ring1", "s2_ring1", "s1_ring2", "s2_ring2")}
    recvs = ("gather_a", "share", "h_yg", "h_a2", "h_r", "h_p", "h_y", "h_g", "x_pp", "x_yy", "x_gc", "x_fin")
    recvs = {name: recv.take() for name in recvs + ("s1_ring1", "s2_ring1", "s1_ring2", "s2_ring2", "s1_relay", "s2_relay")}
    recvs["gather_b"] = recv.take(n)
    for name, parts in (("s1_pair", len(GROUPS[0])), ("s2_pair", len(GROUPS[1]))):
        sends[name] = send.take()
        recvs[name] = recv.take(parts)
    locals_ = {name: local.take() for name in ("w", "y1", "g2", "a2", "a1", "mid", "fresh", "top", "last1", "fo", "bo")}
    return sends, recvs, locals_, send.count, recv.count, local.count


def kernel(
    n, segments, height, width, channels, scale,
    fwd, bwd, fresh, top, w,
    fwd_out, bwd_out, grad_out,
    tf, tb, pp, yy, gc, halo, n2, r1, dx1, out_a, out_b, out_c,
    s_y, s_g, s_a, s_r, s_p, s_y2, s_g2,
    wa, wr, pm, pmt, q2, rows_f32,
    g_1, g_2, pair_send, pair_recv, sum_send, relayed, ring1, fold, ring2_send, ring2, res2, fin,
    send, recv, local,
):
    sends, recvs, locals_ = plan(n)[:3]
    far = n // 2 - 1
    pixels = height * width
    half = channels // 2
    block = 2 * n
    seg = lax.axis_index("segment")
    dp = lax.axis_index("dp")
    core = dp % 2
    chip = dp // 2
    py = chip // n
    pz = chip % n
    first = jnp.where(core == 0, py, pz)
    second = jnp.where(core == 0, pz, py)
    last = segments - 1

    def at(f, g):
        y = jnp.where(core == 0, f, g)
        z = jnp.where(core == 0, g, f)
        return (seg, (y * n + z) * 2 + core)

    partner = (seg, dp + 1 - 2 * core)

    def remote(send_name, recv_name, src, dst, device, recv_slot=0):
        return pltpu.make_async_remote_copy(
            src_ref=src,
            dst_ref=dst,
            send_sem=send.at[sends[send_name]],
            recv_sem=recv.at[recvs[recv_name] + recv_slot],
            device_id=device,
            device_id_type=pl.DeviceIdType.MESH,
        )

    def arrived(recv_name, ref, recv_slot=0):
        remote("halo", recv_name, ref, ref, partner, recv_slot).wait_recv()

    def sent(send_name, ref):
        remote(send_name, "share", ref, ref, partner).wait_send()

    def copy(name, src, dst):
        return pltpu.make_async_copy(src, dst, local.at[locals_[name]])

    def when(flag):
        return pl.when(flag)

    has_next = seg < last
    has_prev = seg > 0
    is_first = seg == 0
    is_last = seg == last

    load_w = copy("w", w, wa.at[second])
    load_y1 = copy("y1", bwd.at[0], tb.at[0])
    load_g2 = copy("g2", bwd.at[3], tb.at[3])
    load_a2 = copy("a2", fwd.at[1], tf.at[1])
    load_a1 = copy("a1", fwd.at[0], tf.at[0])
    load_mid = copy("mid", bwd.at[1:3], tb.at[1:3])
    load_fresh = copy("fresh", fresh, pp)
    load_top = copy("top", top, gc)
    load_last = copy("last1", fwd.at[1], yy.at[0])

    barrier = pltpu.get_barrier_semaphore()

    def greet(device):
        pl.semaphore_signal(barrier, inc=1, device_id=device, device_id_type=pl.DeviceIdType.MESH)

    for i in offsets_of(n):
        greet(at((first + i) % n, second))
        greet(at(first, (second + i) % n))
    greet(partner)

    @when(has_next)
    def _():
        greet((seg + 1, dp))
        greet((seg + 1, partner[1]))

    @when(has_prev)
    def _():
        greet((seg - 1, dp))
        greet((seg - 1, partner[1]))

    for c in (load_w, load_y1, load_g2, load_a2, load_a1, load_mid):
        c.start()

    @when(is_first)
    def _():
        load_fresh.start()

    @when(is_last)
    def _():
        load_top.start()
        load_last.start()

    def natural(k):
        c, f, g, kk = k // half, (k // block) % n, (k // 2) % n, k % 2
        even = f * (4 * n) + g * 4 + kk
        odd = g * (4 * n) + f * 4 + 2 + kk
        return jnp.where(c == 0, even, odd)

    def one_hot(flag):
        return jnp.where(flag, 1.0, 0.0).astype(BF16)

    shape = (channels, channels)
    rows = lax.broadcasted_iota(jnp.int32, shape, 0)
    cols = lax.broadcasted_iota(jnp.int32, shape, 1)
    pm[...] = one_hot(rows == natural(cols))
    pmt[...] = one_hot(natural(rows) == cols)
    shape = (block * TAP_ROWS, block * TAP_ROWS)
    rows = lax.broadcasted_iota(jnp.int32, shape, 0)
    cols = lax.broadcasted_iota(jnp.int32, shape, 1)
    q2[...] = one_hot(
        (rows // (2 * TAP_ROWS) == (cols % block) // 2)
        & ((rows // 2) % TAP_ROWS == cols // block)
        & (rows % 2 == cols % 2)
    )
    fold[...] = jnp.zeros_like(fold)

    def matmul(a, b):
        return jnp.dot(a, b, preferred_element_type=F32)

    def build(dest, tile, edge, permute, relu):
        received = edge[...].astype(F32)
        above = jnp.where(core == 1, received, 0.0).astype(BF16)
        below = jnp.where(core == 0, received, 0.0).astype(BF16)
        whole = jnp.concatenate([above, tile[...].reshape(pixels, channels), below], axis=0)
        value = matmul(whole, pm[...]) if permute else whole.astype(F32)
        if relu:
            value = jnp.maximum(value, 0.0)
        total = pixels + 2 * width
        column = lax.broadcasted_iota(jnp.int32, (total, 1), 0) % width
        full = (height + 2, width, channels)
        dest[1] = value.astype(BF16).reshape(full)
        dest[0] = jnp.where(column == 0, 0.0, pltpu.roll(value, 1, 0)).astype(BF16).reshape(full)
        dest[2] = (
            jnp.where(column == width - 1, 0.0, pltpu.roll(value, total - 1, 0)).astype(BF16).reshape(full)
        )

    def window(s, row_off, col_off):
        return s[col_off, row_off : row_off + height].reshape(pixels, channels)

    def conv(s):
        total = None
        for t in range(TAPS):
            term = matmul(window(s, t // 3, t % 3), wr[t])
            total = term if total is None else total + term
        return total

    def conv_back(s):
        total = None
        for t in range(TAPS):
            term = lax.dot_general(
                window(s, 2 - t // 3, 2 - t % 3), wr[t], (((1,), (1,)), ((), ())), preferred_element_type=F32
            )
            total = term if total is None else total + term
        return total

    def weight_terms(dest, s, cotangent, add, t):
        flat = cotangent[...].reshape(pixels, channels)
        term = lax.dot_general(
            window(s, t // 3, t % 3), flat, (((0,), (0,)), ((), ())), preferred_element_type=F32
        )
        dest[t] = dest[t] + term if add else term

    def flat32(tile):
        return tile[...].reshape(pixels, channels).astype(F32)

    def as_tile(value):
        return value.astype(BF16).reshape(height, width, channels)

    def cot_rebuilt(cot_first, s_kept, s_cot):
        moved = matmul(cot_first[...].reshape(pixels, channels), pm[...])
        kept = s_kept[1, 1 : 1 + height].reshape(pixels, channels).astype(F32)
        total = moved + jnp.where(kept > 0, conv_back(s_cot), 0.0)
        return as_tile(matmul(total.astype(BF16), pmt[...]))

    load_w.wait()
    load_y1.wait()
    load_g2.wait()
    load_a2.wait()
    neighbours = 2 * (n - 1) + 1 + 2 * has_next.astype(jnp.int32) + 2 * has_prev.astype(jnp.int32)
    pl.semaphore_wait(barrier, neighbours)

    for i in offsets_of(n):
        remote("gather_a", "gather_a", wa.at[second], wa.at[second], at(first, (second + i) % n)).start()

    edge_row = jnp.where(core == 0, height - 1, 0)
    remote("halo", "h_yg", tb.at[0, edge_row], halo.at[1], partner).start()
    remote("halo", "h_yg", tb.at[3, edge_row], halo.at[2], partner).start()
    remote("halo", "h_a2", tf.at[1, edge_row], halo.at[0], partner).start()

    ahead = (seg + 1, dp)
    ahead_partner = (seg + 1, partner[1])
    behind = (seg - 1, dp)
    behind_partner = (seg - 1, partner[1])

    @when(has_prev)
    def _():
        remote("x_back", "x_yy", tb.at[0], yy.at[1], behind).start()
        remote("x_back", "x_gc", tb.at[3], gc.at[0], behind).start()

    @when(has_next)
    def _():
        remote("x_ahead", "x_pp", tf.at[1], pp.at[0], ahead).start()

    @when(is_first)
    def _():
        load_fresh.wait()
        remote("edge", "h_p", pp.at[1, edge_row], halo.at[3], partner).start()

    @when(is_last)
    def _():
        load_top.wait()
        load_last.wait()
        remote("edge", "h_y", tf.at[1, edge_row], halo.at[4], partner).start()
        remote("edge", "h_g", gc.at[1, edge_row], halo.at[5], partner).start()

    other_half = pl.multiple_of((1 - core) * half, half)
    own_half = pl.multiple_of(core * half, half)
    own_block = pl.multiple_of(first * block, block)

    def block_rows(f):
        return pl.ds(pl.multiple_of(f * block, block), block)

    def scatter(k, g):
        tag = f"s{k + 1}_"
        relay_taps = ((slice(0, SPLIT), 1), (slice(SPLIT, TAPS), -1))

        def pair_start(part):
            lo, hi = GROUPS[k][part]
            pair_send[k, lo:hi] = g[lo:hi, pl.ds(other_half, half), :].astype(BF16)
            src, dst = pair_send.at[k, lo:hi], pair_recv.at[k, lo:hi]
            remote(tag + "pair", tag + "pair", src, dst, partner, part).start()

        def pair_sum():
            for part, (lo, hi) in enumerate(GROUPS[k]):
                arrived(tag + "pair", pair_recv.at[k, lo:hi], part)
                own = g[lo:hi, pl.ds(own_half, half), :]
                sum_send[k, lo:hi] = (own + pair_recv[k, lo:hi].astype(F32)).astype(BF16)

        def ring_send(i):
            peer = (first + n + i) % n
            src = sum_send.at[k, :, block_rows(peer)]
            remote(tag + "ring1", tag + "ring1", src, ring1.at[k, first], at(peer, second)).start()

        def ring1_near():
            if far > 0:
                for taps, way in relay_taps:
                    src = sum_send.at[k, taps, block_rows((first + n // 2) % n)]
                    dst = relayed.at[k, taps]
                    device = at((first + n + way) % n, second)
                    remote(tag + "ring1", tag + "relay", src, dst, device).start()
                for i in range(far - 1, 0, -1):
                    ring_send(i)
                    ring_send(-i)
            else:
                ring_send(1)

        def ring1_far():
            if far > 0:
                arrived(tag + "relay", relayed.at[k])
                for taps, way in relay_taps:
                    rows = block_rows((first + n + way * far) % n)
                    own = sum_send[k, taps, rows, :].astype(F32)
                    sum_send[k, taps, rows, :] = (own + relayed[k, taps].astype(F32)).astype(BF16)
                ring_send(far)
                ring_send(-far)

        def ring2_start():
            total = sum_send[k, :, pl.ds(own_block, block), :].astype(F32)
            near = [i for i in range(1, n) if far == 0 or i != n // 2]
            arrived(tag + "ring1", ring1.at[k, 0 : len(near)])
            for i in near:
                total = total + ring1[k, (first + i) % n].astype(F32)
            fold[0:TAPS] = total.astype(BF16)
            sorted_rows = matmul(q2[...], fold[...].reshape(TAP_ROWS * block, channels))
            ring2_send[k] = sorted_rows.astype(BF16).reshape(n, 2 * TAP_ROWS, channels)
            for i in offsets_of(n):
                peer = (second + i) % n
                src, dst = ring2_send.at[k, peer], ring2.at[k, second]
                remote(tag + "ring2", tag + "ring2", src, dst, at(first, peer)).start()

        def ring2_sum():
            total = ring2_send[k, second].astype(F32)
            arrived(tag + "ring2", ring2.at[k, 0 : n - 1])
            for i in range(1, n):
                total = total + ring2[k, (second + i) % n].astype(F32)
            return total[0 : 2 * TAPS + 6]

        def finish():
            sent(tag + "pair", pair_send.at[k])
            sent(tag + "ring1", sum_send.at[k, :, 0 : (n - 1) * block])
            sent(tag + "ring2", ring2_send.at[k, 0 : n - 1])

        return pair_start, pair_sum, ring1_near, ring1_far, ring2_start, ring2_sum, finish

    one_pair, one_sum, one_near, one_far, one_ring2, one_total, one_finish = scatter(0, g_1)
    two_pair, two_sum, two_near, two_far, two_ring2, two_total, two_finish = scatter(1, g_2)

    arrived("h_yg", halo.at[1:3])
    build(s_y, tb.at[0], halo.at[1], True, True)
    build(s_g, tb.at[3], halo.at[2], False, False)

    def weight_rows(c, f):
        return pl.ds(pl.multiple_of(c * half + f * block, block), block)

    arrived("gather_a", wa.at[0 : n - 1])
    for g in range(n):
        for t in range(TAPS):
            rows_f32[t * block + 2 * g : t * block + 2 * g + 2, :] = wa[g, t].astype(F32)
    mine = weight_rows(core, first)
    wr[:, mine, :] = rows_f32[...].astype(BF16).reshape(TAPS, block, channels)

    def weight_send(src, way, taps, slot):
        ref = wr.at[taps, weight_rows(core, src)]
        remote("gather_b", "gather_b", ref, ref, at((first + n + way) % n, second), slot).start()

    def share(f):
        ref = wr.at[:, weight_rows(core, f)]
        remote("share", "share", ref, ref, partner).start()

    def weights_from(f):
        arrived("gather_b", wr.at[:, weight_rows(core, f)], f)

    every = slice(0, TAPS)
    reach = range(far, 0, -1) if far > 0 else [1]
    for i in reach:
        weight_send(first, i, every, first)
        if far > 0:
            weight_send(first, -i, every, first)
    share(first)

    for t in range(TAPS):
        weight_terms(g_1, s_y, tb.at[3], False, t)
    arrived("h_a2", halo.at[0])
    build(s_a, tf.at[1], halo.at[0], True, True)

    @when(is_last)
    def _():
        for t in range(TAPS):
            weight_terms(g_1, s_a, gc.at[1], True, t)

    one_pair(0)

    opposite = (first + n // 2) % n
    if far > 0:
        for way in (1, -1):
            origin = (first + n + way * far) % n
            weights_from(origin)
            taps = slice(0, SPLIT) if way > 0 else slice(SPLIT, TAPS)
            receiver = (first + n - way) % n
            slot = origin if way > 0 else receiver
            weight_send(origin, -way, taps, slot)
            share(origin)
        for i in range(1, far):
            for way in (1, -1):
                origin = (first + n + way * i) % n
                weights_from(origin)
                share(origin)
        arrived("gather_b", wr.at[0:SPLIT, weight_rows(core, opposite)], opposite)
        arrived("gather_b", wr.at[SPLIT:TAPS, weight_rows(core, opposite)], first)
    else:
        weights_from(opposite)
    share(opposite)
    one_sum()
    arrived("share", wr.at[:, pl.ds(other_half, half)])
    one_near()

    load_mid.wait()
    r1[...] = as_tile(flat32(tb.at[1]) - conv(s_y))

    @when(has_prev)
    def _():
        remote("x_back_row", "h_r", r1.at[edge_row], halo.at[6], partner).start()
        remote("x_back_row", "h_y", r1.at[edge_row], halo.at[4], behind_partner).start()
        remote("x_back", "x_yy", r1, yy.at[0], behind).start()

    dx1[...] = cot_rebuilt(tb.at[2], s_y, s_g)

    @when(has_prev)
    def _():
        remote("x_back_row", "h_g", dx1.at[edge_row], halo.at[5], behind_partner).start()
        remote("x_back", "x_gc", dx1, gc.at[1], behind).start()

    one_far()

    @when(has_prev)
    def _():
        arrived("h_r", halo.at[6])
        build(s_r, r1, halo.at[6], True, True)
        for part, (lo, hi) in enumerate(GROUPS[1]):
            for t in range(lo, hi):
                weight_terms(g_2, s_r, dx1, False, t)
            two_pair(part)

    load_a1.wait()
    n2[...] = as_tile(flat32(tf.at[0]) + conv(s_a))

    @when(has_next)
    def _():
        remote("x_ahead_row", "h_p", n2.at[edge_row], halo.at[3], ahead_partner).start()
        remote("x_ahead", "x_pp", n2, pp.at[1], ahead).start()

    @when(is_last)
    def _():
        yy[1] = n2[...]

    @when(has_prev)
    def _():
        two_sum()
        two_near()
        two_far()

    arrived("h_y", halo.at[4])

    @when(has_next)
    def _():
        arrived("x_yy", yy)

    build(s_y2, yy.at[0], halo.at[4], True, True)
    out_b[...] = as_tile(flat32(yy.at[1]) - conv(s_y2))
    copy("bo", out_b, bwd_out.at[0]).start()
    copy("bo", yy.at[0], bwd_out.at[1]).start()

    one_ring2()

    arrived("h_p", halo.at[3])

    @when(has_prev)
    def _():
        arrived("x_pp", pp)

    build(s_p, pp.at[1], halo.at[3], True, True)
    out_a[...] = as_tile(flat32(pp.at[0]) + conv(s_p))
    copy("fo", pp.at[1], fwd_out.at[0]).start()
    copy("fo", out_a, fwd_out.at[1]).start()

    @when(has_prev)
    def _():
        two_ring2()

    arrived("h_g", halo.at[5])

    @when(has_next)
    def _():
        arrived("x_gc", gc)

    build(s_g2, gc.at[1], halo.at[5], False, False)
    out_c[...] = cot_rebuilt(gc.at[0], s_y2, s_g2)
    copy("bo", gc.at[1], bwd_out.at[2]).start()
    copy("bo", out_c, bwd_out.at[3]).start()
    rows_f32[0 : 2 * TAPS + 6, :] = one_total()

    @when(has_prev)
    def _():
        res2[...] = two_total()
        remote("x_fin", "x_fin", res2, fin, behind).start()

    @when(has_next)
    def _():
        arrived("x_fin", fin)
        rows_f32[0 : 2 * TAPS + 6, :] = rows_f32[0 : 2 * TAPS + 6, :] + fin[...]

    for t in range(TAPS):
        grad_out[t] = rows_f32[2 * t : 2 * t + 2, :] * scale

    sent("gather_a", wa.at[0 : n - 1])
    sent("gather_b", wr.at[:, 0 : (n - 1) * block])
    sent("share", wr.at[:, pl.ds(other_half, half)])
    sent("halo", halo.at[0:3])
    one_finish()

    @when(has_prev)
    def _():
        sent("x_back", tb)
        sent("x_back_row", halo.at[0:3])
        sent("x_fin", fin)
        two_finish()

    @when(has_next)
    def _():
        sent("x_ahead", tf)
        sent("x_ahead_row", halo.at[0])

    @when(is_first)
    def _():
        sent("edge", halo.at[0])

    @when(is_last)
    def _():
        sent("edge", halo.at[0:2])

    copy("fo", fwd_out, fwd_out).wait()
    copy("bo", bwd_out, bwd_out).wait()


def fused(n, segments, scale, fwd, bwd, fresh, top, w):
    height, width, channels = fwd.shape[1:]
    tile = (height, width, channels)
    shifted = (3, height + 2, width, channels)
    half = channels // 2
    block = 2 * n
    n_send, n_recv, n_local = plan(n)[3:]
    square = (channels, channels)
    mixed = (block * TAP_ROWS, block * TAP_ROWS)
    v = pltpu.VMEM
    scratch = [
        v((2, *tile), BF16),
        v((4, *tile), BF16),
        v((2, *tile), BF16),
        v((2, *tile), BF16),
        v((2, *tile), BF16),
        v((7, width, channels), BF16),
        v(tile, BF16),
        v(tile, BF16),
        v(tile, BF16),
        v(tile, BF16),
        v(tile, BF16),
        v(tile, BF16),
        *[v(shifted, BF16)] * 7,
        v((n, TAPS, 2, channels), BF16),
        v((TAPS, channels, channels), BF16),
        v(square, BF16),
        v(square, BF16),
        v(mixed, BF16),
        v((max(TAPS * block, 2 * TAPS + 6), channels), F32),
        v((TAPS, channels, channels), F32),
        v((TAPS, channels, channels), F32),
        v((2, TAPS, half, channels), BF16),
        v((2, TAPS, half, channels), BF16),
        v((2, TAPS, half, channels), BF16),
        v((2, TAPS, block, channels), BF16),
        v((2, n, TAPS, block, channels), BF16),
        v((TAP_ROWS, block, channels), BF16),
        v((2, n, 2 * TAP_ROWS, channels), BF16),
        v((2, n, 2 * TAP_ROWS, channels), BF16),
        v((2 * TAPS + 6, channels), F32),
        v((2 * TAPS + 6, channels), F32),
        pltpu.SemaphoreType.DMA((n_send,)),
        pltpu.SemaphoreType.DMA((n_recv,)),
        pltpu.SemaphoreType.DMA((n_local,)),
    ]
    return pl.pallas_call(
        functools.partial(kernel, n, segments, height, width, channels, scale),
        out_shape=(
            jax.ShapeDtypeStruct((2, *tile), BF16),
            jax.ShapeDtypeStruct((4, *tile), BF16),
            jax.ShapeDtypeStruct((TAPS, 2, channels), F32),
        ),
        in_specs=[pl.BlockSpec(memory_space=pltpu.HBM)] * 5,
        out_specs=(
            pl.BlockSpec(memory_space=pl.ANY),
            pl.BlockSpec(memory_space=pl.ANY),
            pl.BlockSpec(memory_space=pltpu.VMEM),
        ),
        scratch_shapes=scratch,
        compiler_params=pltpu.CompilerParams(collective_id=0, has_side_effects=True, vmem_limit_bytes=44 << 20),
        name="coupling",
    )(*[pltpu.with_memory_space_constraint(x, pltpu.HBM) for x in (fwd, bwd, fresh, top, w)])


def place_kernel(a, b, c, a_out, b_out, c_out, sems):
    copies = [
        pltpu.make_async_copy(src, dst, sems.at[i])
        for i, (src, dst) in enumerate(((b, b_out), (a, a_out), (c, c_out)))
    ]
    for c in copies:
        c.start()
    for c in copies:
        c.wait()


def placed(arrays):
    return pl.pallas_call(
        place_kernel,
        out_shape=tuple(jax.ShapeDtypeStruct(x.shape, x.dtype) for x in arrays),
        in_specs=[pl.BlockSpec(memory_space=pl.ANY)] * 3,
        out_specs=(pl.BlockSpec(memory_space=pl.ANY),) * 3,
        scratch_shapes=[pltpu.SemaphoreType.DMA((3,))],
        compiler_params=pltpu.CompilerParams(vmem_limit_bytes=8 << 20),
        name="place",
    )(*arrays)


def shards(segments, tiles, fwd_in, bwd_in, fresh, top_cot, conv_weight):
    height, width, channels = fwd_in.shape[3:]
    n = math.isqrt(tiles // 2)
    scale = (2.0 * tiles * height * width) ** (-0.5)
    weight = conv_weight[0].transpose(1, 0, 2)
    results = fused(
        n, segments, scale, fwd_in[:, 0, 0], bwd_in[:, 0, 0], fresh[:, 0], top_cot[:, 0], weight
    )
    forward, message, grad = placed(results)
    return forward[:, None, None], message[:, None, None], grad.transpose(1, 0, 2)[None]


def solution(mesh):
    segments = mesh.shape["segment"]
    tiles = mesh.shape["dp"]
    streams = P(None, "segment", "dp", None, None, None)
    halves = P(None, "dp", None, None, None)
    weights = P("segment", "dp", None, None)
    return jax.shard_map(
        functools.partial(shards, segments, tiles),
        mesh=mesh,
        in_specs=(streams, streams, halves, halves, weights),
        out_specs=(streams, streams, weights),
        check_vma=False,
    )
```

```python
import functools
import math

import jax
import jax.numpy as jnp
from jax import lax
from jax.experimental import pallas as pl
from jax.experimental.pallas import tpu as pltpu
from jax.sharding import PartitionSpec as P

F32 = jnp.float32
BF16 = jnp.bfloat16
TAPS = 9
TAP_ROWS = 16
GROUPS = (((0, 9),), ((0, 3), (3, 6), (6, 9)))
SPLIT = 5


class Sems:
    def __init__(self):
        self.count = 0

    def take(self, amount=1):
        first = self.count
        self.count += amount
        return first


def offsets_of(n):
    return sorted(range(1, n), key=lambda i: -min(i, n - i))


def plan(n):
    send, recv, local = Sems(), Sems(), Sems()
    sends = ("gather_a", "gather_b", "share", "halo", "edge", "x_back", "x_back_row", "x_ahead", "x_ahead_row", "x_fin")
    sends = {name: send.take() for name in sends + ("s1_ring1", "s2_ring1", "s1_ring2", "s2_ring2")}
    recvs = ("gather_a", "share", "h_yg", "h_a2", "h_r", "h_p", "h_y", "h_g", "x_pp", "x_yy", "x_gc", "x_fin")
    recvs = {name: recv.take() for name in recvs + ("s1_ring1", "s2_ring1", "s1_ring2", "s2_ring2", "s1_full", "s2_full", "s1_part", "s2_part")}
    recvs["gather_b"] = recv.take(n)
    for name, parts in (("s1_pair", len(GROUPS[0])), ("s2_pair", len(GROUPS[1]))):
        sends[name] = send.take()
        recvs[name] = recv.take(parts)
    locals_ = {name: local.take() for name in ("w", "y1", "g2", "a2", "a1", "mid", "fresh", "top", "last1", "fo", "bo")}
    return sends, recvs, locals_, send.count, recv.count, local.count


def kernel(
    n, segments, height, width, channels, scale,
    fwd, bwd, fresh, top, w,
    fwd_out, bwd_out, grad_out,
    tf, tb, pp, yy, gc, halo, n2, r1, dx1, out_a, out_b, out_c,
    s_y, s_g, s_a, s_r, s_p, s_y2, s_g2,
    wa, wr, pm, pmt, q2, rows_f32,
    g_1, g_2, pair_send, pair_recv, sum_send, full, part_, ring1, fold, ring2_send, ring2, res2, fin,
    send, recv, local,
):
    sends, recvs, locals_ = plan(n)[:3]
    hop = n // 4
    beyond = range(hop + 1, n // 2) if hop > 0 else range(0)
    pixels = height * width
    half = channels // 2
    block = 2 * n
    seg = lax.axis_index("segment")
    dp = lax.axis_index("dp")
    core = dp % 2
    chip = dp // 2
    py = chip // n
    pz = chip % n
    first = jnp.where(core == 0, py, pz)
    second = jnp.where(core == 0, pz, py)
    last = segments - 1

    def at(f, g):
        y = jnp.where(core == 0, f, g)
        z = jnp.where(core == 0, g, f)
        return (seg, (y * n + z) * 2 + core)

    partner = (seg, dp + 1 - 2 * core)

    def remote(send_name, recv_name, src, dst, device, recv_slot=0):
        return pltpu.make_async_remote_copy(
            src_ref=src,
            dst_ref=dst,
            send_sem=send.at[sends[send_name]],
            recv_sem=recv.at[recvs[recv_name] + recv_slot],
            device_id=device,
            device_id_type=pl.DeviceIdType.MESH,
        )

    def arrived(recv_name, ref, recv_slot=0):
        remote("halo", recv_name, ref, ref, partner, recv_slot).wait_recv()

    def sent(send_name, ref):
        remote(send_name, "share", ref, ref, partner).wait_send()

    def copy(name, src, dst):
        return pltpu.make_async_copy(src, dst, local.at[locals_[name]])

    def when(flag):
        return pl.when(flag)

    has_next = seg < last
    has_prev = seg > 0
    is_first = seg == 0
    is_last = seg == last

    load_w = copy("w", w, wa.at[second])
    load_y1 = copy("y1", bwd.at[0], tb.at[0])
    load_g2 = copy("g2", bwd.at[3], tb.at[3])
    load_a2 = copy("a2", fwd.at[1], tf.at[1])
    load_a1 = copy("a1", fwd.at[0], tf.at[0])
    load_mid = copy("mid", bwd.at[1:3], tb.at[1:3])
    load_fresh = copy("fresh", fresh, pp)
    load_top = copy("top", top, gc)
    load_last = copy("last1", fwd.at[1], yy.at[0])

    barrier = pltpu.get_barrier_semaphore()

    def greet(device):
        pl.semaphore_signal(barrier, inc=1, device_id=device, device_id_type=pl.DeviceIdType.MESH)

    for i in offsets_of(n):
        greet(at((first + i) % n, second))
        greet(at(first, (second + i) % n))
    greet(partner)

    @when(has_next)
    def _():
        greet((seg + 1, dp))
        greet((seg + 1, partner[1]))

    @when(has_prev)
    def _():
        greet((seg - 1, dp))
        greet((seg - 1, partner[1]))

    for c in (load_w, load_y1, load_g2, load_a2, load_a1, load_mid):
        c.start()

    @when(is_first)
    def _():
        load_fresh.start()

    @when(is_last)
    def _():
        load_top.start()
        load_last.start()

    def natural(k):
        c, f, g, kk = k // half, (k // block) % n, (k // 2) % n, k % 2
        even = f * (4 * n) + g * 4 + kk
        odd = g * (4 * n) + f * 4 + 2 + kk
        return jnp.where(c == 0, even, odd)

    def one_hot(flag):
        return jnp.where(flag, 1.0, 0.0).astype(BF16)

    shape = (channels, channels)
    rows = lax.broadcasted_iota(jnp.int32, shape, 0)
    cols = lax.broadcasted_iota(jnp.int32, shape, 1)
    pm[...] = one_hot(rows == natural(cols))
    pmt[...] = one_hot(natural(rows) == cols)
    shape = (block * TAP_ROWS, block * TAP_ROWS)
    rows = lax.broadcasted_iota(jnp.int32, shape, 0)
    cols = lax.broadcasted_iota(jnp.int32, shape, 1)
    q2[...] = one_hot(
        (rows // (2 * TAP_ROWS) == (cols % block) // 2)
        & ((rows // 2) % TAP_ROWS == cols // block)
        & (rows % 2 == cols % 2)
    )
    fold[...] = jnp.zeros_like(fold)

    def matmul(a, b):
        return jnp.dot(a, b, preferred_element_type=F32)

    def build(dest, tile, edge, permute, relu):
        received = edge[...].astype(F32)
        above = jnp.where(core == 1, received, 0.0).astype(BF16)
        below = jnp.where(core == 0, received, 0.0).astype(BF16)
        whole = jnp.concatenate([above, tile[...].reshape(pixels, channels), below], axis=0)
        value = matmul(whole, pm[...]) if permute else whole.astype(F32)
        if relu:
            value = jnp.maximum(value, 0.0)
        total = pixels + 2 * width
        column = lax.broadcasted_iota(jnp.int32, (total, 1), 0) % width
        full = (height + 2, width, channels)
        dest[1] = value.astype(BF16).reshape(full)
        dest[0] = jnp.where(column == 0, 0.0, pltpu.roll(value, 1, 0)).astype(BF16).reshape(full)
        dest[2] = (
            jnp.where(column == width - 1, 0.0, pltpu.roll(value, total - 1, 0)).astype(BF16).reshape(full)
        )

    def window(s, row_off, col_off):
        return s[col_off, row_off : row_off + height].reshape(pixels, channels)

    def conv(s):
        total = None
        for t in range(TAPS):
            term = matmul(window(s, t // 3, t % 3), wr[t])
            total = term if total is None else total + term
        return total

    def conv_back(s):
        total = None
        for t in range(TAPS):
            term = lax.dot_general(
                window(s, 2 - t // 3, 2 - t % 3), wr[t], (((1,), (1,)), ((), ())), preferred_element_type=F32
            )
            total = term if total is None else total + term
        return total

    def weight_terms(dest, s, cotangent, add, t):
        flat = cotangent[...].reshape(pixels, channels)
        term = lax.dot_general(
            window(s, t // 3, t % 3), flat, (((0,), (0,)), ((), ())), preferred_element_type=F32
        )
        dest[t] = dest[t] + term if add else term

    def flat32(tile):
        return tile[...].reshape(pixels, channels).astype(F32)

    def as_tile(value):
        return value.astype(BF16).reshape(height, width, channels)

    def cot_rebuilt(cot_first, s_kept, s_cot):
        moved = matmul(cot_first[...].reshape(pixels, channels), pm[...])
        kept = s_kept[1, 1 : 1 + height].reshape(pixels, channels).astype(F32)
        total = moved + jnp.where(kept > 0, conv_back(s_cot), 0.0)
        return as_tile(matmul(total.astype(BF16), pmt[...]))

    load_w.wait()
    load_y1.wait()
    load_g2.wait()
    load_a2.wait()
    neighbours = 2 * (n - 1) + 1 + 2 * has_next.astype(jnp.int32) + 2 * has_prev.astype(jnp.int32)
    pl.semaphore_wait(barrier, neighbours)

    for i in offsets_of(n):
        remote("gather_a", "gather_a", wa.at[second], wa.at[second], at(first, (second + i) % n)).start()

    edge_row = jnp.where(core == 0, height - 1, 0)
    remote("halo", "h_yg", tb.at[0, edge_row], halo.at[1], partner).start()
    remote("halo", "h_yg", tb.at[3, edge_row], halo.at[2], partner).start()
    remote("halo", "h_a2", tf.at[1, edge_row], halo.at[0], partner).start()

    ahead = (seg + 1, dp)
    ahead_partner = (seg + 1, partner[1])
    behind = (seg - 1, dp)
    behind_partner = (seg - 1, partner[1])

    @when(has_prev)
    def _():
        remote("x_back", "x_yy", tb.at[0], yy.at[1], behind).start()
        remote("x_back", "x_gc", tb.at[3], gc.at[0], behind).start()

    @when(has_next)
    def _():
        remote("x_ahead", "x_pp", tf.at[1], pp.at[0], ahead).start()

    @when(is_first)
    def _():
        load_fresh.wait()
        remote("edge", "h_p", pp.at[1, edge_row], halo.at[3], partner).start()

    @when(is_last)
    def _():
        load_top.wait()
        load_last.wait()
        remote("edge", "h_y", tf.at[1, edge_row], halo.at[4], partner).start()
        remote("edge", "h_g", gc.at[1, edge_row], halo.at[5], partner).start()

    other_half = pl.multiple_of((1 - core) * half, half)
    own_half = pl.multiple_of(core * half, half)
    own_block = pl.multiple_of(first * block, block)

    def block_rows(f):
        return pl.ds(pl.multiple_of(f * block, block), block)

    def scatter(k, g):
        tag = f"s{k + 1}_"
        ways = ((1, slice(0, SPLIT)), (-1, slice(SPLIT, TAPS)))

        def pair_start(part):
            lo, hi = GROUPS[k][part]
            pair_send[k, lo:hi] = g[lo:hi, pl.ds(other_half, half), :].astype(BF16)
            src, dst = pair_send.at[k, lo:hi], pair_recv.at[k, lo:hi]
            remote(tag + "pair", tag + "pair", src, dst, partner, part).start()

        def pair_sum():
            for part, (lo, hi) in enumerate(GROUPS[k]):
                arrived(tag + "pair", pair_recv.at[k, lo:hi], part)
                own = g[lo:hi, pl.ds(own_half, half), :]
                sum_send[k, lo:hi] = (own + pair_recv[k, lo:hi].astype(F32)).astype(BF16)

        def away(i):
            return (first + n + i) % n

        def ring_send(way, i):
            slot = 2 * (i - 1) + (0 if way > 0 else 1)
            src = sum_send.at[k, :, block_rows(away(way * i))]
            remote(tag + "ring1", tag + "ring1", src, ring1.at[k, slot], at(away(way * i), second)).start()

        def ring1_near():
            if hop == 0:
                ring_send(1, 1)
                return
            for way, taps in ways:
                for e in beyond:
                    src = sum_send.at[k, :, block_rows(away(way * e))]
                    dst = full.at[k, 2 * (e - hop - 1) + (0 if way > 0 else 1)]
                    remote(tag + "ring1", tag + "full", src, dst, at(away(way * (e - hop)), second)).start()
            for way, taps in ways:
                src = sum_send.at[k, taps, block_rows(away(n // 2))]
                device = at(away(way * (n // 2 - hop)), second)
                remote(tag + "ring1", tag + "part", src, part_.at[k, taps], device).start()
            for i in range(1, hop):
                for way, _ in ways:
                    ring_send(way, i)

        def ring1_far():
            if hop == 0:
                return
            if len(beyond) > 0:
                arrived(tag + "full", full.at[k])
            arrived(tag + "part", part_.at[k])
            for way, taps in ways:
                rows = block_rows(away(way * hop))
                total = sum_send[k, :, rows, :].astype(F32)
                for e in beyond:
                    total = total + full[k, 2 * (e - hop - 1) + (0 if way > 0 else 1)].astype(F32)
                sum_send[k, :, rows, :] = total.astype(BF16)
                own = total[taps] + part_[k, taps].astype(F32)
                sum_send[k, taps, rows, :] = own.astype(BF16)
                ring_send(way, hop)

        def ring2_start():
            total = sum_send[k, :, pl.ds(own_block, block), :].astype(F32)
            slots = 2 * hop if hop > 0 else 1
            arrived(tag + "ring1", ring1.at[k])
            for i in range(slots):
                total = total + ring1[k, i].astype(F32)
            fold[0:TAPS] = total.astype(BF16)
            sorted_rows = matmul(q2[...], fold[...].reshape(TAP_ROWS * block, channels))
            ring2_send[k] = sorted_rows.astype(BF16).reshape(n, 2 * TAP_ROWS, channels)
            for i in offsets_of(n):
                peer = (second + i) % n
                src, dst = ring2_send.at[k, peer], ring2.at[k, second]
                remote(tag + "ring2", tag + "ring2", src, dst, at(first, peer)).start()

        def ring2_sum():
            total = ring2_send[k, second].astype(F32)
            arrived(tag + "ring2", ring2.at[k, 0 : n - 1])
            for i in range(1, n):
                total = total + ring2[k, (second + i) % n].astype(F32)
            return total[0 : 2 * TAPS + 6]

        def finish():
            sent(tag + "pair", pair_send.at[k])
            sent(tag + "ring1", sum_send.at[k, :, 0 : (n - 1) * block])
            sent(tag + "ring2", ring2_send.at[k, 0 : n - 1])

        return pair_start, pair_sum, ring1_near, ring1_far, ring2_start, ring2_sum, finish

    one_pair, one_sum, one_near, one_far, one_ring2, one_total, one_finish = scatter(0, g_1)
    two_pair, two_sum, two_near, two_far, two_ring2, two_total, two_finish = scatter(1, g_2)

    arrived("h_yg", halo.at[1:3])
    build(s_y, tb.at[0], halo.at[1], True, True)
    build(s_g, tb.at[3], halo.at[2], False, False)

    def weight_rows(c, f):
        return pl.ds(pl.multiple_of(c * half + f * block, block), block)

    arrived("gather_a", wa.at[0 : n - 1])
    for g in range(n):
        for t in range(TAPS):
            rows_f32[t * block + 2 * g : t * block + 2 * g + 2, :] = wa[g, t].astype(F32)
    mine = weight_rows(core, first)
    wr[:, mine, :] = rows_f32[...].astype(BF16).reshape(TAPS, block, channels)

    def weight_send(src, way, taps, slot):
        ref = wr.at[taps, weight_rows(core, src)]
        remote("gather_b", "gather_b", ref, ref, at((first + n + way) % n, second), slot).start()

    def share(f):
        ref = wr.at[:, weight_rows(core, f)]
        remote("share", "share", ref, ref, partner).start()

    def weights_from(f):
        arrived("gather_b", wr.at[:, weight_rows(core, f)], f)

    every = slice(0, TAPS)
    for i in range(max(hop, 1), 0, -1):
        weight_send(first, i, every, first)
        if hop > 0:
            weight_send(first, -i, every, first)
    share(first)

    for t in range(TAPS):
        weight_terms(g_1, s_y, tb.at[3], False, t)
    arrived("h_a2", halo.at[0])
    build(s_a, tf.at[1], halo.at[0], True, True)

    @when(is_last)
    def _():
        for t in range(TAPS):
            weight_terms(g_1, s_a, gc.at[1], True, t)

    one_pair(0)

    opposite = (first + n // 2) % n
    if hop > 0:
        for way in (1, -1):
            origin = (first + n - way * hop) % n
            weights_from(origin)
            for e in beyond:
                weight_send(origin, way * (e - hop), every, origin)
            taps = slice(0, SPLIT) if way > 0 else slice(SPLIT, TAPS)
            receiver = (first + n + way * (n // 2 - hop)) % n
            slot = origin if way > 0 else receiver
            weight_send(origin, way * (n // 2 - hop), taps, slot)
            share(origin)
        for i in [*range(1, hop), *beyond]:
            for way in (1, -1):
                origin = (first + n - way * i) % n
                weights_from(origin)
                share(origin)
        arrived("gather_b", wr.at[0:SPLIT, weight_rows(core, opposite)], opposite)
        arrived("gather_b", wr.at[SPLIT:TAPS, weight_rows(core, opposite)], first)
    else:
        weights_from(opposite)
    share(opposite)
    one_sum()
    arrived("share", wr.at[:, pl.ds(other_half, half)])
    one_near()

    load_mid.wait()
    r1[...] = as_tile(flat32(tb.at[1]) - conv(s_y))

    @when(has_prev)
    def _():
        remote("x_back_row", "h_r", r1.at[edge_row], halo.at[6], partner).start()
        remote("x_back_row", "h_y", r1.at[edge_row], halo.at[4], behind_partner).start()
        remote("x_back", "x_yy", r1, yy.at[0], behind).start()

    dx1[...] = cot_rebuilt(tb.at[2], s_y, s_g)

    @when(has_prev)
    def _():
        remote("x_back_row", "h_g", dx1.at[edge_row], halo.at[5], behind_partner).start()
        remote("x_back", "x_gc", dx1, gc.at[1], behind).start()

    one_far()

    @when(has_prev)
    def _():
        arrived("h_r", halo.at[6])
        build(s_r, r1, halo.at[6], True, True)
        for part, (lo, hi) in enumerate(GROUPS[1]):
            for t in range(lo, hi):
                weight_terms(g_2, s_r, dx1, False, t)
            two_pair(part)

    load_a1.wait()
    n2[...] = as_tile(flat32(tf.at[0]) + conv(s_a))

    @when(has_next)
    def _():
        remote("x_ahead_row", "h_p", n2.at[edge_row], halo.at[3], ahead_partner).start()
        remote("x_ahead", "x_pp", n2, pp.at[1], ahead).start()

    @when(is_last)
    def _():
        yy[1] = n2[...]

    @when(has_prev)
    def _():
        two_sum()
        two_near()
        two_far()

    arrived("h_y", halo.at[4])

    @when(has_next)
    def _():
        arrived("x_yy", yy)

    build(s_y2, yy.at[0], halo.at[4], True, True)
    out_b[...] = as_tile(flat32(yy.at[1]) - conv(s_y2))
    copy("bo", out_b, bwd_out.at[0]).start()
    copy("bo", yy.at[0], bwd_out.at[1]).start()

    one_ring2()

    arrived("h_p", halo.at[3])

    @when(has_prev)
    def _():
        arrived("x_pp", pp)

    build(s_p, pp.at[1], halo.at[3], True, True)
    out_a[...] = as_tile(flat32(pp.at[0]) + conv(s_p))
    copy("fo", pp.at[1], fwd_out.at[0]).start()
    copy("fo", out_a, fwd_out.at[1]).start()

    @when(has_prev)
    def _():
        two_ring2()

    arrived("h_g", halo.at[5])

    @when(has_next)
    def _():
        arrived("x_gc", gc)

    build(s_g2, gc.at[1], halo.at[5], False, False)
    out_c[...] = cot_rebuilt(gc.at[0], s_y2, s_g2)
    copy("bo", gc.at[1], bwd_out.at[2]).start()
    copy("bo", out_c, bwd_out.at[3]).start()
    rows_f32[0 : 2 * TAPS + 6, :] = one_total()

    @when(has_prev)
    def _():
        res2[...] = two_total()
        remote("x_fin", "x_fin", res2, fin, behind).start()

    @when(has_next)
    def _():
        arrived("x_fin", fin)
        rows_f32[0 : 2 * TAPS + 6, :] = rows_f32[0 : 2 * TAPS + 6, :] + fin[...]

    for t in range(TAPS):
        grad_out[t] = rows_f32[2 * t : 2 * t + 2, :] * scale

    sent("gather_a", wa.at[0 : n - 1])
    sent("gather_b", wr.at[:, 0 : (n - 1) * block])
    sent("share", wr.at[:, pl.ds(other_half, half)])
    sent("halo", halo.at[0:3])
    one_finish()

    @when(has_prev)
    def _():
        sent("x_back", tb)
        sent("x_back_row", halo.at[0:3])
        sent("x_fin", fin)
        two_finish()

    @when(has_next)
    def _():
        sent("x_ahead", tf)
        sent("x_ahead_row", halo.at[0])

    @when(is_first)
    def _():
        sent("edge", halo.at[0])

    @when(is_last)
    def _():
        sent("edge", halo.at[0:2])

    copy("fo", fwd_out, fwd_out).wait()
    copy("bo", bwd_out, bwd_out).wait()


def fused(n, segments, scale, fwd, bwd, fresh, top, w):
    height, width, channels = fwd.shape[1:]
    tile = (height, width, channels)
    shifted = (3, height + 2, width, channels)
    half = channels // 2
    block = 2 * n
    n_send, n_recv, n_local = plan(n)[3:]
    square = (channels, channels)
    mixed = (block * TAP_ROWS, block * TAP_ROWS)
    v = pltpu.VMEM
    scratch = [
        v((2, *tile), BF16),
        v((4, *tile), BF16),
        v((2, *tile), BF16),
        v((2, *tile), BF16),
        v((2, *tile), BF16),
        v((7, width, channels), BF16),
        v(tile, BF16),
        v(tile, BF16),
        v(tile, BF16),
        v(tile, BF16),
        v(tile, BF16),
        v(tile, BF16),
        *[v(shifted, BF16)] * 7,
        v((n, TAPS, 2, channels), BF16),
        v((TAPS, channels, channels), BF16),
        v(square, BF16),
        v(square, BF16),
        v(mixed, BF16),
        v((max(TAPS * block, 2 * TAPS + 6), channels), F32),
        v((TAPS, channels, channels), F32),
        v((TAPS, channels, channels), F32),
        v((2, TAPS, half, channels), BF16),
        v((2, TAPS, half, channels), BF16),
        v((2, TAPS, half, channels), BF16),
        v((2, 2 * max(n // 2 - 1 - n // 4, 1), TAPS, block, channels), BF16),
        v((2, TAPS, block, channels), BF16),
        v((2, max(2 * (n // 4), 1), TAPS, block, channels), BF16),
        v((TAP_ROWS, block, channels), BF16),
        v((2, n, 2 * TAP_ROWS, channels), BF16),
        v((2, n, 2 * TAP_ROWS, channels), BF16),
        v((2 * TAPS + 6, channels), F32),
        v((2 * TAPS + 6, channels), F32),
        pltpu.SemaphoreType.DMA((n_send,)),
        pltpu.SemaphoreType.DMA((n_recv,)),
        pltpu.SemaphoreType.DMA((n_local,)),
    ]
    return pl.pallas_call(
        functools.partial(kernel, n, segments, height, width, channels, scale),
        out_shape=(
            jax.ShapeDtypeStruct((2, *tile), BF16),
            jax.ShapeDtypeStruct((4, *tile), BF16),
            jax.ShapeDtypeStruct((TAPS, 2, channels), F32),
        ),
        in_specs=[pl.BlockSpec(memory_space=pltpu.HBM)] * 5,
        out_specs=(
            pl.BlockSpec(memory_space=pl.ANY),
            pl.BlockSpec(memory_space=pl.ANY),
            pl.BlockSpec(memory_space=pltpu.VMEM),
        ),
        scratch_shapes=scratch,
        compiler_params=pltpu.CompilerParams(collective_id=0, has_side_effects=True, vmem_limit_bytes=44 << 20),
        name="coupling",
    )(*[pltpu.with_memory_space_constraint(x, pltpu.HBM) for x in (fwd, bwd, fresh, top, w)])


def place_kernel(a, b, c, a_out, b_out, c_out, sems):
    copies = [
        pltpu.make_async_copy(src, dst, sems.at[i])
        for i, (src, dst) in enumerate(((b, b_out), (a, a_out), (c, c_out)))
    ]
    for c in copies:
        c.start()
    for c in copies:
        c.wait()


def placed(arrays):
    return pl.pallas_call(
        place_kernel,
        out_shape=tuple(jax.ShapeDtypeStruct(x.shape, x.dtype) for x in arrays),
        in_specs=[pl.BlockSpec(memory_space=pl.ANY)] * 3,
        out_specs=(pl.BlockSpec(memory_space=pl.ANY),) * 3,
        scratch_shapes=[pltpu.SemaphoreType.DMA((3,))],
        compiler_params=pltpu.CompilerParams(vmem_limit_bytes=8 << 20),
        name="place",
    )(*arrays)


def shards(segments, tiles, fwd_in, bwd_in, fresh, top_cot, conv_weight):
    height, width, channels = fwd_in.shape[3:]
    n = math.isqrt(tiles // 2)
    scale = (2.0 * tiles * height * width) ** (-0.5)
    weight = conv_weight[0].transpose(1, 0, 2)
    results = fused(
        n, segments, scale, fwd_in[:, 0, 0], bwd_in[:, 0, 0], fresh[:, 0], top_cot[:, 0], weight
    )
    forward, message, grad = placed(results)
    return forward[:, None, None], message[:, None, None], grad.transpose(1, 0, 2)[None]


def solution(mesh):
    segments = mesh.shape["segment"]
    tiles = mesh.shape["dp"]
    streams = P(None, "segment", "dp", None, None, None)
    halves = P(None, "dp", None, None, None)
    weights = P("segment", "dp", None, None)
    return jax.shard_map(
        functools.partial(shards, segments, tiles),
        mesh=mesh,
        in_specs=(streams, streams, halves, halves, weights),
        out_specs=(streams, streams, weights),
        check_vma=False,
    )
```

```python
import functools
import math

import jax
import jax.numpy as jnp
from jax import lax
from jax.experimental import pallas as pl
from jax.experimental.pallas import tpu as pltpu
from jax.sharding import PartitionSpec as P

F32 = jnp.float32
BF16 = jnp.bfloat16
TAPS = 9
TAP_ROWS = 16
GROUPS = (((0, 9),), ((0, 3), (3, 6), (6, 9)))
SPLIT = 5


class Sems:
    def __init__(self):
        self.count = 0

    def take(self, amount=1):
        first = self.count
        self.count += amount
        return first


def offsets_of(n):
    return sorted(range(1, n), key=lambda i: -min(i, n - i))


def plan(n):
    send, recv, local = Sems(), Sems(), Sems()
    sends = ("gather_a", "gather_b", "share", "halo", "edge", "x_back", "x_back_row", "x_ahead", "x_ahead_row", "x_fin")
    sends = {name: send.take() for name in sends + ("s1_ring1", "s2_ring1", "s1_ring2", "s2_ring2")}
    recvs = ("gather_a", "share", "h_yg", "h_a2", "h_r", "h_p", "h_y", "h_g", "x_pp", "x_yy", "x_gc", "x_fin")
    recvs = {name: recv.take() for name in recvs + ("s1_ring1", "s2_ring1", "s1_ring2", "s2_ring2", "s1_relay", "s2_relay")}
    recvs["gather_b"] = recv.take(n)
    for name, parts in (("s1_pair", len(GROUPS[0])), ("s2_pair", len(GROUPS[1]))):
        sends[name] = send.take()
        recvs[name] = recv.take(parts)
    locals_ = {name: local.take() for name in ("w", "y1", "g2", "a2", "a1", "mid", "fresh", "top", "last1", "fo", "bo")}
    return sends, recvs, locals_, send.count, recv.count, local.count


def kernel(
    n, segments, height, width, channels, scale,
    fwd, bwd, fresh, top, w,
    fwd_out, bwd_out, grad_out,
    tf, tb, pp, yy, gc, halo, n2, r1, dx1, out_a, out_b, out_c,
    s_y, s_g, s_a, s_r, s_p, s_y2, s_g2,
    wa, wr, pm, pmt, q2, rows_f32,
    g_1, g_2, pair_send, pair_recv, sum_send, relayed, ring1, fold, ring2_send, ring2, res2, fin,
    send, recv, local,
):
    sends, recvs, locals_ = plan(n)[:3]
    far = n // 2 - 1
    pixels = height * width
    half = channels // 2
    block = 2 * n
    seg = lax.axis_index("segment")
    dp = lax.axis_index("dp")
    core = dp % 2
    chip = dp // 2
    py = chip // n
    pz = chip % n
    first = jnp.where(core == 0, py, pz)
    second = jnp.where(core == 0, pz, py)
    last = segments - 1

    def at(f, g):
        y = jnp.where(core == 0, f, g)
        z = jnp.where(core == 0, g, f)
        return (seg, (y * n + z) * 2 + core)

    partner = (seg, dp + 1 - 2 * core)

    def remote(send_name, recv_name, src, dst, device, recv_slot=0):
        return pltpu.make_async_remote_copy(
            src_ref=src,
            dst_ref=dst,
            send_sem=send.at[sends[send_name]],
            recv_sem=recv.at[recvs[recv_name] + recv_slot],
            device_id=device,
            device_id_type=pl.DeviceIdType.MESH,
        )

    def arrived(recv_name, ref, recv_slot=0):
        remote("halo", recv_name, ref, ref, partner, recv_slot).wait_recv()

    def sent(send_name, ref):
        remote(send_name, "share", ref, ref, partner).wait_send()

    def copy(name, src, dst):
        return pltpu.make_async_copy(src, dst, local.at[locals_[name]])

    def when(flag):
        return pl.when(flag)

    has_next = seg < last
    has_prev = seg > 0
    is_first = seg == 0
    is_last = seg == last

    load_w = copy("w", w, wa.at[second])
    load_y1 = copy("y1", bwd.at[0], tb.at[0])
    load_g2 = copy("g2", bwd.at[3], tb.at[3])
    load_a2 = copy("a2", fwd.at[1], tf.at[1])
    load_a1 = copy("a1", fwd.at[0], tf.at[0])
    load_mid = copy("mid", bwd.at[1:3], tb.at[1:3])
    load_fresh = copy("fresh", fresh, pp)
    load_top = copy("top", top, gc)
    load_last = copy("last1", fwd.at[1], yy.at[0])

    barrier = pltpu.get_barrier_semaphore()

    def greet(device):
        pl.semaphore_signal(barrier, inc=1, device_id=device, device_id_type=pl.DeviceIdType.MESH)

    for i in offsets_of(n):
        greet(at((first + i) % n, second))
        greet(at(first, (second + i) % n))
    greet(partner)

    @when(has_next)
    def _():
        greet((seg + 1, dp))
        greet((seg + 1, partner[1]))

    @when(has_prev)
    def _():
        greet((seg - 1, dp))
        greet((seg - 1, partner[1]))

    for c in (load_w, load_y1, load_g2, load_a2, load_a1, load_mid):
        c.start()

    @when(is_first)
    def _():
        load_fresh.start()

    @when(is_last)
    def _():
        load_top.start()
        load_last.start()

    def natural(k):
        c, f, g, kk = k // half, (k // block) % n, (k // 2) % n, k % 2
        even = f * (4 * n) + g * 4 + kk
        odd = g * (4 * n) + f * 4 + 2 + kk
        return jnp.where(c == 0, even, odd)

    def one_hot(flag):
        return jnp.where(flag, 1.0, 0.0).astype(BF16)

    shape = (channels, channels)
    rows = lax.broadcasted_iota(jnp.int32, shape, 0)
    cols = lax.broadcasted_iota(jnp.int32, shape, 1)
    pm[...] = one_hot(rows == natural(cols))
    pmt[...] = one_hot(natural(rows) == cols)
    shape = (block * TAP_ROWS, block * TAP_ROWS)
    rows = lax.broadcasted_iota(jnp.int32, shape, 0)
    cols = lax.broadcasted_iota(jnp.int32, shape, 1)
    q2[...] = one_hot(
        (rows // (2 * TAP_ROWS) == (cols % block) // 2)
        & ((rows // 2) % TAP_ROWS == cols // block)
        & (rows % 2 == cols % 2)
    )
    fold[...] = jnp.zeros_like(fold)

    def matmul(a, b):
        return jnp.dot(a, b, preferred_element_type=F32)

    def build(dest, tile, edge, permute, relu):
        received = edge[...].astype(F32)
        above = jnp.where(core == 1, received, 0.0).astype(BF16)
        below = jnp.where(core == 0, received, 0.0).astype(BF16)
        whole = jnp.concatenate([above, tile[...].reshape(pixels, channels), below], axis=0)
        value = matmul(whole, pm[...]) if permute else whole.astype(F32)
        if relu:
            value = jnp.maximum(value, 0.0)
        total = pixels + 2 * width
        column = lax.broadcasted_iota(jnp.int32, (total, 1), 0) % width
        full = (height + 2, width, channels)
        dest[1] = value.astype(BF16).reshape(full)
        dest[0] = jnp.where(column == 0, 0.0, pltpu.roll(value, 1, 0)).astype(BF16).reshape(full)
        dest[2] = (
            jnp.where(column == width - 1, 0.0, pltpu.roll(value, total - 1, 0)).astype(BF16).reshape(full)
        )

    def window(s, row_off, col_off):
        return s[col_off, row_off : row_off + height].reshape(pixels, channels)

    def conv(s):
        total = None
        for t in range(TAPS):
            term = matmul(window(s, t // 3, t % 3), wr[t])
            total = term if total is None else total + term
        return total

    def conv_back(s):
        total = None
        for t in range(TAPS):
            term = lax.dot_general(
                window(s, 2 - t // 3, 2 - t % 3), wr[t], (((1,), (1,)), ((), ())), preferred_element_type=F32
            )
            total = term if total is None else total + term
        return total

    def weight_terms(dest, s, cotangent, add, t):
        flat = cotangent[...].reshape(pixels, channels)
        term = lax.dot_general(
            window(s, t // 3, t % 3), flat, (((0,), (0,)), ((), ())), preferred_element_type=F32
        )
        dest[t] = dest[t] + term if add else term

    def flat32(tile):
        return tile[...].reshape(pixels, channels).astype(F32)

    def as_tile(value):
        return value.astype(BF16).reshape(height, width, channels)

    def cot_rebuilt(cot_first, s_kept, s_cot):
        moved = matmul(cot_first[...].reshape(pixels, channels), pm[...])
        kept = s_kept[1, 1 : 1 + height].reshape(pixels, channels).astype(F32)
        total = moved + jnp.where(kept > 0, conv_back(s_cot), 0.0)
        return as_tile(matmul(total.astype(BF16), pmt[...]))

    load_w.wait()
    load_y1.wait()
    load_g2.wait()
    load_a2.wait()
    neighbours = 2 * (n - 1) + 1 + 2 * has_next.astype(jnp.int32) + 2 * has_prev.astype(jnp.int32)
    pl.semaphore_wait(barrier, neighbours)

    for i in offsets_of(n):
        remote("gather_a", "gather_a", wa.at[second], wa.at[second], at(first, (second + i) % n)).start()

    edge_row = jnp.where(core == 0, height - 1, 0)
    remote("halo", "h_yg", tb.at[0, edge_row], halo.at[1], partner).start()
    remote("halo", "h_yg", tb.at[3, edge_row], halo.at[2], partner).start()
    remote("halo", "h_a2", tf.at[1, edge_row], halo.at[0], partner).start()

    ahead = (seg + 1, dp)
    ahead_partner = (seg + 1, partner[1])
    behind = (seg - 1, dp)
    behind_partner = (seg - 1, partner[1])

    @when(has_prev)
    def _():
        remote("x_back", "x_yy", tb.at[0], yy.at[1], behind).start()
        remote("x_back", "x_gc", tb.at[3], gc.at[0], behind).start()

    @when(has_next)
    def _():
        remote("x_ahead", "x_pp", tf.at[1], pp.at[0], ahead).start()

    @when(is_first)
    def _():
        load_fresh.wait()
        remote("edge", "h_p", pp.at[1, edge_row], halo.at[3], partner).start()

    @when(is_last)
    def _():
        load_top.wait()
        load_last.wait()
        remote("edge", "h_y", tf.at[1, edge_row], halo.at[4], partner).start()
        remote("edge", "h_g", gc.at[1, edge_row], halo.at[5], partner).start()

    other_half = pl.multiple_of((1 - core) * half, half)
    own_half = pl.multiple_of(core * half, half)
    own_block = pl.multiple_of(first * block, block)

    def block_rows(f):
        return pl.ds(pl.multiple_of(f * block, block), block)

    def scatter(k, g):
        tag = f"s{k + 1}_"
        relay_taps = ((slice(0, SPLIT), 1), (slice(SPLIT, TAPS), -1))

        def pair_start(part):
            lo, hi = GROUPS[k][part]
            pair_send[k, lo:hi] = g[lo:hi, pl.ds(other_half, half), :].astype(BF16)
            src, dst = pair_send.at[k, lo:hi], pair_recv.at[k, lo:hi]
            remote(tag + "pair", tag + "pair", src, dst, partner, part).start()

        def pair_sum():
            for part, (lo, hi) in enumerate(GROUPS[k]):
                arrived(tag + "pair", pair_recv.at[k, lo:hi], part)
                own = g[lo:hi, pl.ds(own_half, half), :]
                sum_send[k, lo:hi] = (own + pair_recv[k, lo:hi].astype(F32)).astype(BF16)

        def ring_send(i):
            peer = (first + n + i) % n
            src = sum_send.at[k, :, block_rows(peer)]
            remote(tag + "ring1", tag + "ring1", src, ring1.at[k, first], at(peer, second)).start()

        relay = k == 1 and far > 0

        def ring1_near():
            if relay:
                for taps, way in relay_taps:
                    src = sum_send.at[k, taps, block_rows((first + n // 2) % n)]
                    dst = relayed.at[k, taps]
                    device = at((first + n + way) % n, second)
                    remote(tag + "ring1", tag + "relay", src, dst, device).start()
                for i in range(far - 1, 0, -1):
                    ring_send(i)
                    ring_send(-i)
            else:
                for i in offsets_of(n):
                    ring_send(i)

        def ring1_far():
            if relay:
                arrived(tag + "relay", relayed.at[k])
                for taps, way in relay_taps:
                    rows = block_rows((first + n + way * far) % n)
                    own = sum_send[k, taps, rows, :].astype(F32)
                    sum_send[k, taps, rows, :] = (own + relayed[k, taps].astype(F32)).astype(BF16)
                ring_send(far)
                ring_send(-far)

        def ring2_start():
            total = sum_send[k, :, pl.ds(own_block, block), :].astype(F32)
            near = [i for i in range(1, n) if not relay or i != n // 2]
            arrived(tag + "ring1", ring1.at[k, 0 : len(near)])
            for i in near:
                total = total + ring1[k, (first + i) % n].astype(F32)
            fold[0:TAPS] = total.astype(BF16)
            sorted_rows = matmul(q2[...], fold[...].reshape(TAP_ROWS * block, channels))
            ring2_send[k] = sorted_rows.astype(BF16).reshape(n, 2 * TAP_ROWS, channels)
            for i in offsets_of(n):
                peer = (second + i) % n
                src, dst = ring2_send.at[k, peer], ring2.at[k, second]
                remote(tag + "ring2", tag + "ring2", src, dst, at(first, peer)).start()

        def ring2_sum():
            total = ring2_send[k, second].astype(F32)
            arrived(tag + "ring2", ring2.at[k, 0 : n - 1])
            for i in range(1, n):
                total = total + ring2[k, (second + i) % n].astype(F32)
            return total[0 : 2 * TAPS + 6]

        def finish():
            sent(tag + "pair", pair_send.at[k])
            sent(tag + "ring1", sum_send.at[k, :, 0 : (n - 1) * block])
            sent(tag + "ring2", ring2_send.at[k, 0 : n - 1])

        return pair_start, pair_sum, ring1_near, ring1_far, ring2_start, ring2_sum, finish

    one_pair, one_sum, one_near, _, one_ring2, one_total, one_finish = scatter(0, g_1)
    two_pair, two_sum, two_near, two_far, two_ring2, two_total, two_finish = scatter(1, g_2)

    arrived("h_yg", halo.at[1:3])
    build(s_y, tb.at[0], halo.at[1], True, True)
    build(s_g, tb.at[3], halo.at[2], False, False)

    def weight_rows(c, f):
        return pl.ds(pl.multiple_of(c * half + f * block, block), block)

    arrived("gather_a", wa.at[0 : n - 1])
    for g in range(n):
        for t in range(TAPS):
            rows_f32[t * block + 2 * g : t * block + 2 * g + 2, :] = wa[g, t].astype(F32)
    mine = weight_rows(core, first)
    wr[:, mine, :] = rows_f32[...].astype(BF16).reshape(TAPS, block, channels)

    def weight_send(src, way, taps, slot):
        ref = wr.at[taps, weight_rows(core, src)]
        remote("gather_b", "gather_b", ref, ref, at((first + n + way) % n, second), slot).start()

    def share(f):
        ref = wr.at[:, weight_rows(core, f)]
        remote("share", "share", ref, ref, partner).start()

    def weights_from(f):
        arrived("gather_b", wr.at[:, weight_rows(core, f)], f)

    every = slice(0, TAPS)
    reach = range(far, 0, -1) if far > 0 else [1]
    for i in reach:
        weight_send(first, i, every, first)
        if far > 0:
            weight_send(first, -i, every, first)
    share(first)

    for t in range(TAPS):
        weight_terms(g_1, s_y, tb.at[3], False, t)
    arrived("h_a2", halo.at[0])
    build(s_a, tf.at[1], halo.at[0], True, True)

    @when(is_last)
    def _():
        for t in range(TAPS):
            weight_terms(g_1, s_a, gc.at[1], True, t)

    one_pair(0)

    opposite = (first + n // 2) % n
    if far > 0:
        for way in (1, -1):
            origin = (first + n + way * far) % n
            weights_from(origin)
            taps = slice(0, SPLIT) if way > 0 else slice(SPLIT, TAPS)
            receiver = (first + n - way) % n
            slot = origin if way > 0 else receiver
            weight_send(origin, -way, taps, slot)
            share(origin)
        for i in range(1, far):
            for way in (1, -1):
                origin = (first + n + way * i) % n
                weights_from(origin)
                share(origin)
        arrived("gather_b", wr.at[0:SPLIT, weight_rows(core, opposite)], opposite)
        arrived("gather_b", wr.at[SPLIT:TAPS, weight_rows(core, opposite)], first)
    else:
        weights_from(opposite)
    share(opposite)
    one_sum()
    one_near()
    arrived("share", wr.at[:, pl.ds(other_half, half)])

    load_mid.wait()
    r1[...] = as_tile(flat32(tb.at[1]) - conv(s_y))

    @when(has_prev)
    def _():
        remote("x_back_row", "h_r", r1.at[edge_row], halo.at[6], partner).start()
        remote("x_back_row", "h_y", r1.at[edge_row], halo.at[4], behind_partner).start()
        remote("x_back", "x_yy", r1, yy.at[0], behind).start()

    dx1[...] = cot_rebuilt(tb.at[2], s_y, s_g)

    @when(has_prev)
    def _():
        remote("x_back_row", "h_g", dx1.at[edge_row], halo.at[5], behind_partner).start()
        remote("x_back", "x_gc", dx1, gc.at[1], behind).start()

        arrived("h_r", halo.at[6])
        build(s_r, r1, halo.at[6], True, True)
        for part, (lo, hi) in enumerate(GROUPS[1]):
            for t in range(lo, hi):
                weight_terms(g_2, s_r, dx1, False, t)
            two_pair(part)

    load_a1.wait()
    n2[...] = as_tile(flat32(tf.at[0]) + conv(s_a))

    @when(has_next)
    def _():
        remote("x_ahead_row", "h_p", n2.at[edge_row], halo.at[3], ahead_partner).start()
        remote("x_ahead", "x_pp", n2, pp.at[1], ahead).start()

    @when(is_last)
    def _():
        yy[1] = n2[...]

    @when(has_prev)
    def _():
        two_sum()
        two_near()
        two_far()

    arrived("h_y", halo.at[4])

    @when(has_next)
    def _():
        arrived("x_yy", yy)

    build(s_y2, yy.at[0], halo.at[4], True, True)
    out_b[...] = as_tile(flat32(yy.at[1]) - conv(s_y2))
    copy("bo", out_b, bwd_out.at[0]).start()
    copy("bo", yy.at[0], bwd_out.at[1]).start()

    one_ring2()

    arrived("h_p", halo.at[3])

    @when(has_prev)
    def _():
        arrived("x_pp", pp)

    build(s_p, pp.at[1], halo.at[3], True, True)
    out_a[...] = as_tile(flat32(pp.at[0]) + conv(s_p))
    copy("fo", pp.at[1], fwd_out.at[0]).start()
    copy("fo", out_a, fwd_out.at[1]).start()

    @when(has_prev)
    def _():
        two_ring2()

    arrived("h_g", halo.at[5])

    @when(has_next)
    def _():
        arrived("x_gc", gc)

    build(s_g2, gc.at[1], halo.at[5], False, False)
    out_c[...] = cot_rebuilt(gc.at[0], s_y2, s_g2)
    copy("bo", gc.at[1], bwd_out.at[2]).start()
    copy("bo", out_c, bwd_out.at[3]).start()
    rows_f32[0 : 2 * TAPS + 6, :] = one_total()

    @when(has_prev)
    def _():
        res2[...] = two_total()
        remote("x_fin", "x_fin", res2, fin, behind).start()

    @when(has_next)
    def _():
        arrived("x_fin", fin)
        rows_f32[0 : 2 * TAPS + 6, :] = rows_f32[0 : 2 * TAPS + 6, :] + fin[...]

    for t in range(TAPS):
        grad_out[t] = rows_f32[2 * t : 2 * t + 2, :] * scale

    sent("gather_a", wa.at[0 : n - 1])
    sent("gather_b", wr.at[:, 0 : (n - 1) * block])
    sent("share", wr.at[:, pl.ds(other_half, half)])
    sent("halo", halo.at[0:3])
    one_finish()

    @when(has_prev)
    def _():
        sent("x_back", tb)
        sent("x_back_row", halo.at[0:3])
        sent("x_fin", fin)
        two_finish()

    @when(has_next)
    def _():
        sent("x_ahead", tf)
        sent("x_ahead_row", halo.at[0])

    @when(is_first)
    def _():
        sent("edge", halo.at[0])

    @when(is_last)
    def _():
        sent("edge", halo.at[0:2])

    copy("fo", fwd_out, fwd_out).wait()
    copy("bo", bwd_out, bwd_out).wait()


def fused(n, segments, scale, fwd, bwd, fresh, top, w):
    height, width, channels = fwd.shape[1:]
    tile = (height, width, channels)
    shifted = (3, height + 2, width, channels)
    half = channels // 2
    block = 2 * n
    n_send, n_recv, n_local = plan(n)[3:]
    square = (channels, channels)
    mixed = (block * TAP_ROWS, block * TAP_ROWS)
    v = pltpu.VMEM
    scratch = [
        v((2, *tile), BF16),
        v((4, *tile), BF16),
        v((2, *tile), BF16),
        v((2, *tile), BF16),
        v((2, *tile), BF16),
        v((7, width, channels), BF16),
        v(tile, BF16),
        v(tile, BF16),
        v(tile, BF16),
        v(tile, BF16),
        v(tile, BF16),
        v(tile, BF16),
        *[v(shifted, BF16)] * 7,
        v((n, TAPS, 2, channels), BF16),
        v((TAPS, channels, channels), BF16),
        v(square, BF16),
        v(square, BF16),
        v(mixed, BF16),
        v((max(TAPS * block, 2 * TAPS + 6), channels), F32),
        v((TAPS, channels, channels), F32),
        v((TAPS, channels, channels), F32),
        v((2, TAPS, half, channels), BF16),
        v((2, TAPS, half, channels), BF16),
        v((2, TAPS, half, channels), BF16),
        v((2, TAPS, block, channels), BF16),
        v((2, n, TAPS, block, channels), BF16),
        v((TAP_ROWS, block, channels), BF16),
        v((2, n, 2 * TAP_ROWS, channels), BF16),
        v((2, n, 2 * TAP_ROWS, channels), BF16),
        v((2 * TAPS + 6, channels), F32),
        v((2 * TAPS + 6, channels), F32),
        pltpu.SemaphoreType.DMA((n_send,)),
        pltpu.SemaphoreType.DMA((n_recv,)),
        pltpu.SemaphoreType.DMA((n_local,)),
    ]
    return pl.pallas_call(
        functools.partial(kernel, n, segments, height, width, channels, scale),
        out_shape=(
            jax.ShapeDtypeStruct((2, *tile), BF16),
            jax.ShapeDtypeStruct((4, *tile), BF16),
            jax.ShapeDtypeStruct((TAPS, 2, channels), F32),
        ),
        in_specs=[pl.BlockSpec(memory_space=pltpu.HBM)] * 5,
        out_specs=(
            pl.BlockSpec(memory_space=pl.ANY),
            pl.BlockSpec(memory_space=pl.ANY),
            pl.BlockSpec(memory_space=pltpu.VMEM),
        ),
        scratch_shapes=scratch,
        compiler_params=pltpu.CompilerParams(collective_id=0, has_side_effects=True, vmem_limit_bytes=44 << 20),
        name="coupling",
    )(*[pltpu.with_memory_space_constraint(x, pltpu.HBM) for x in (fwd, bwd, fresh, top, w)])


def place_kernel(a, b, c, a_out, b_out, c_out, sems):
    copies = [
        pltpu.make_async_copy(src, dst, sems.at[i])
        for i, (src, dst) in enumerate(((b, b_out), (a, a_out), (c, c_out)))
    ]
    for c in copies:
        c.start()
    for c in copies:
        c.wait()


def placed(arrays):
    return pl.pallas_call(
        place_kernel,
        out_shape=tuple(jax.ShapeDtypeStruct(x.shape, x.dtype) for x in arrays),
        in_specs=[pl.BlockSpec(memory_space=pl.ANY)] * 3,
        out_specs=(pl.BlockSpec(memory_space=pl.ANY),) * 3,
        scratch_shapes=[pltpu.SemaphoreType.DMA((3,))],
        compiler_params=pltpu.CompilerParams(vmem_limit_bytes=8 << 20),
        name="place",
    )(*arrays)


def shards(segments, tiles, fwd_in, bwd_in, fresh, top_cot, conv_weight):
    height, width, channels = fwd_in.shape[3:]
    n = math.isqrt(tiles // 2)
    scale = (2.0 * tiles * height * width) ** (-0.5)
    weight = conv_weight[0].transpose(1, 0, 2)
    results = fused(
        n, segments, scale, fwd_in[:, 0, 0], bwd_in[:, 0, 0], fresh[:, 0], top_cot[:, 0], weight
    )
    forward, message, grad = placed(results)
    return forward[:, None, None], message[:, None, None], grad.transpose(1, 0, 2)[None]


def solution(mesh):
    segments = mesh.shape["segment"]
    tiles = mesh.shape["dp"]
    streams = P(None, "segment", "dp", None, None, None)
    halves = P(None, "dp", None, None, None)
    weights = P("segment", "dp", None, None)
    return jax.shard_map(
        functools.partial(shards, segments, tiles),
        mesh=mesh,
        in_specs=(streams, streams, halves, halves, weights),
        out_specs=(streams, streams, weights),
        check_vma=False,
    )
```

```python
import functools
import math

import jax
import jax.numpy as jnp
from jax import lax
from jax.experimental import pallas as pl
from jax.experimental.pallas import tpu as pltpu
from jax.sharding import PartitionSpec as P

F32 = jnp.float32
BF16 = jnp.bfloat16
TAPS = 9
TAP_ROWS = 16
GROUPS = (((0, 9),), ((0, 3), (3, 6), (6, 9)))
SPLIT = 5


class Sems:
    def __init__(self):
        self.count = 0

    def take(self, amount=1):
        first = self.count
        self.count += amount
        return first


def offsets_of(n):
    return sorted(range(1, n), key=lambda i: -min(i, n - i))


def plan(n):
    send, recv, local = Sems(), Sems(), Sems()
    sends = ("gather_a", "gather_b", "share", "halo", "edge", "x_back", "x_back_row", "x_ahead", "x_ahead_row", "x_fin")
    sends = {name: send.take() for name in sends + ("s1_ring1", "s2_ring1", "s1_ring2", "s2_ring2")}
    recvs = ("gather_a", "share", "h_yg", "h_a2", "h_r", "h_p", "h_y", "h_g", "x_pp", "x_yy", "x_gc", "x_fin")
    recvs = {name: recv.take() for name in recvs + ("s1_ring1", "s2_ring1", "s1_ring2", "s2_ring2", "s1_relay", "s2_relay")}
    recvs["gather_b"] = recv.take(n)
    for name, parts in (("s1_pair", len(GROUPS[0])), ("s2_pair", len(GROUPS[1]))):
        sends[name] = send.take()
        recvs[name] = recv.take(parts)
    locals_ = {name: local.take() for name in ("w", "y1", "g2", "a2", "a1", "mid", "fresh", "top", "last1", "fo", "bo")}
    return sends, recvs, locals_, send.count, recv.count, local.count


def kernel(
    n, segments, height, width, channels, scale,
    fwd, bwd, fresh, top, w,
    fwd_out, bwd_out, grad_out,
    tf, tb, pp, yy, gc, halo, n2, r1, dx1, out_a, out_b, out_c,
    s_y, s_g, s_a, s_r, s_p, s_y2, s_g2,
    wa, wr, pm, pmt, q2, rows_f32,
    g_1, g_2, pair_send, pair_recv, sum_send, relayed, ring1, fold, ring2_send, ring2, res2, fin,
    send, recv, local,
):
    sends, recvs, locals_ = plan(n)[:3]
    far = n // 2 - 1
    pixels = height * width
    half = channels // 2
    block = 2 * n
    seg = lax.axis_index("segment")
    dp = lax.axis_index("dp")
    core = dp % 2
    chip = dp // 2
    py = chip // n
    pz = chip % n
    first = jnp.where(core == 0, py, pz)
    second = jnp.where(core == 0, pz, py)
    last = segments - 1

    def at(f, g):
        y = jnp.where(core == 0, f, g)
        z = jnp.where(core == 0, g, f)
        return (seg, (y * n + z) * 2 + core)

    partner = (seg, dp + 1 - 2 * core)

    def remote(send_name, recv_name, src, dst, device, recv_slot=0):
        return pltpu.make_async_remote_copy(
            src_ref=src,
            dst_ref=dst,
            send_sem=send.at[sends[send_name]],
            recv_sem=recv.at[recvs[recv_name] + recv_slot],
            device_id=device,
            device_id_type=pl.DeviceIdType.MESH,
        )

    def arrived(recv_name, ref, recv_slot=0):
        remote("halo", recv_name, ref, ref, partner, recv_slot).wait_recv()

    def sent(send_name, ref):
        remote(send_name, "share", ref, ref, partner).wait_send()

    def copy(name, src, dst):
        return pltpu.make_async_copy(src, dst, local.at[locals_[name]])

    def when(flag):
        return pl.when(flag)

    has_next = seg < last
    has_prev = seg > 0
    is_first = seg == 0
    is_last = seg == last

    load_w = copy("w", w, wa.at[second])
    load_y1 = copy("y1", bwd.at[0], tb.at[0])
    load_g2 = copy("g2", bwd.at[3], tb.at[3])
    load_a2 = copy("a2", fwd.at[1], tf.at[1])
    load_a1 = copy("a1", fwd.at[0], tf.at[0])
    load_mid = copy("mid", bwd.at[1:3], tb.at[1:3])
    load_fresh = copy("fresh", fresh, pp)
    load_top = copy("top", top, gc)
    load_last = copy("last1", fwd.at[1], yy.at[0])

    barrier = pltpu.get_barrier_semaphore()

    def greet(device):
        pl.semaphore_signal(barrier, inc=1, device_id=device, device_id_type=pl.DeviceIdType.MESH)

    for i in offsets_of(n):
        greet(at((first + i) % n, second))
        greet(at(first, (second + i) % n))
    greet(partner)

    @when(has_next)
    def _():
        greet((seg + 1, dp))
        greet((seg + 1, partner[1]))

    @when(has_prev)
    def _():
        greet((seg - 1, dp))
        greet((seg - 1, partner[1]))

    for c in (load_w, load_y1, load_g2, load_a2, load_a1, load_mid):
        c.start()

    @when(is_first)
    def _():
        load_fresh.start()

    @when(is_last)
    def _():
        load_top.start()
        load_last.start()

    def natural(k):
        c, f, g, kk = k // half, (k // block) % n, (k // 2) % n, k % 2
        even = f * (4 * n) + g * 4 + kk
        odd = g * (4 * n) + f * 4 + 2 + kk
        return jnp.where(c == 0, even, odd)

    def one_hot(flag):
        return jnp.where(flag, 1.0, 0.0).astype(BF16)

    shape = (channels, channels)
    rows = lax.broadcasted_iota(jnp.int32, shape, 0)
    cols = lax.broadcasted_iota(jnp.int32, shape, 1)
    pm[...] = one_hot(rows == natural(cols))
    pmt[...] = one_hot(natural(rows) == cols)
    shape = (block * TAP_ROWS, block * TAP_ROWS)
    rows = lax.broadcasted_iota(jnp.int32, shape, 0)
    cols = lax.broadcasted_iota(jnp.int32, shape, 1)
    q2[...] = one_hot(
        (rows // (2 * TAP_ROWS) == (cols % block) // 2)
        & ((rows // 2) % TAP_ROWS == cols // block)
        & (rows % 2 == cols % 2)
    )
    fold[...] = jnp.zeros_like(fold)

    def matmul(a, b):
        return jnp.dot(a, b, preferred_element_type=F32)

    def build(dest, tile, edge, permute, relu):
        received = edge[...].astype(F32)
        above = jnp.where(core == 1, received, 0.0).astype(BF16)
        below = jnp.where(core == 0, received, 0.0).astype(BF16)
        whole = jnp.concatenate([above, tile[...].reshape(pixels, channels), below], axis=0)
        value = matmul(whole, pm[...]) if permute else whole.astype(F32)
        if relu:
            value = jnp.maximum(value, 0.0)
        total = pixels + 2 * width
        column = lax.broadcasted_iota(jnp.int32, (total, 1), 0) % width
        full = (height + 2, width, channels)
        dest[1] = value.astype(BF16).reshape(full)
        dest[0] = jnp.where(column == 0, 0.0, pltpu.roll(value, 1, 0)).astype(BF16).reshape(full)
        dest[2] = (
            jnp.where(column == width - 1, 0.0, pltpu.roll(value, total - 1, 0)).astype(BF16).reshape(full)
        )

    def window(s, row_off, col_off):
        return s[col_off, row_off : row_off + height].reshape(pixels, channels)

    def conv(s):
        total = None
        for t in range(TAPS):
            term = matmul(window(s, t // 3, t % 3), wr[t])
            total = term if total is None else total + term
        return total

    def conv_back(s):
        total = None
        for t in range(TAPS):
            term = lax.dot_general(
                window(s, 2 - t // 3, 2 - t % 3), wr[t], (((1,), (1,)), ((), ())), preferred_element_type=F32
            )
            total = term if total is None else total + term
        return total

    def weight_terms(dest, s, cotangent, add, t):
        flat = cotangent[...].reshape(pixels, channels)
        term = lax.dot_general(
            window(s, t // 3, t % 3), flat, (((0,), (0,)), ((), ())), preferred_element_type=F32
        )
        dest[t] = dest[t] + term if add else term

    def flat32(tile):
        return tile[...].reshape(pixels, channels).astype(F32)

    def as_tile(value):
        return value.astype(BF16).reshape(height, width, channels)

    def cot_rebuilt(cot_first, s_kept, s_cot):
        moved = matmul(cot_first[...].reshape(pixels, channels), pm[...])
        kept = s_kept[1, 1 : 1 + height].reshape(pixels, channels).astype(F32)
        total = moved + jnp.where(kept > 0, conv_back(s_cot), 0.0)
        return as_tile(matmul(total.astype(BF16), pmt[...]))

    load_w.wait()
    load_y1.wait()
    load_g2.wait()
    load_a2.wait()
    neighbours = 2 * (n - 1) + 1 + 2 * has_next.astype(jnp.int32) + 2 * has_prev.astype(jnp.int32)
    pl.semaphore_wait(barrier, neighbours)

    for i in offsets_of(n):
        remote("gather_a", "gather_a", wa.at[second], wa.at[second], at(first, (second + i) % n)).start()

    edge_row = jnp.where(core == 0, height - 1, 0)
    remote("halo", "h_yg", tb.at[0, edge_row], halo.at[1], partner).start()
    remote("halo", "h_yg", tb.at[3, edge_row], halo.at[2], partner).start()
    remote("halo", "h_a2", tf.at[1, edge_row], halo.at[0], partner).start()

    ahead = (seg + 1, dp)
    ahead_partner = (seg + 1, partner[1])
    behind = (seg - 1, dp)
    behind_partner = (seg - 1, partner[1])

    @when(has_prev)
    def _():
        remote("x_back", "x_yy", tb.at[0], yy.at[1], behind).start()
        remote("x_back", "x_gc", tb.at[3], gc.at[0], behind).start()

    @when(has_next)
    def _():
        remote("x_ahead", "x_pp", tf.at[1], pp.at[0], ahead).start()

    @when(is_first)
    def _():
        load_fresh.wait()
        remote("edge", "h_p", pp.at[1, edge_row], halo.at[3], partner).start()

    @when(is_last)
    def _():
        load_top.wait()
        load_last.wait()
        remote("edge", "h_y", tf.at[1, edge_row], halo.at[4], partner).start()
        remote("edge", "h_g", gc.at[1, edge_row], halo.at[5], partner).start()

    other_half = pl.multiple_of((1 - core) * half, half)
    own_half = pl.multiple_of(core * half, half)
    own_block = pl.multiple_of(first * block, block)

    def block_rows(f):
        return pl.ds(pl.multiple_of(f * block, block), block)

    def scatter(k, g):
        tag = f"s{k + 1}_"
        relay_taps = ((slice(0, SPLIT), 1), (slice(SPLIT, TAPS), -1))

        def pair_start(part):
            lo, hi = GROUPS[k][part]
            pair_send[k, lo:hi] = g[lo:hi, pl.ds(other_half, half), :].astype(BF16)
            src, dst = pair_send.at[k, lo:hi], pair_recv.at[k, lo:hi]
            remote(tag + "pair", tag + "pair", src, dst, partner, part).start()

        def pair_sum():
            for part, (lo, hi) in enumerate(GROUPS[k]):
                arrived(tag + "pair", pair_recv.at[k, lo:hi], part)
                own = g[lo:hi, pl.ds(own_half, half), :]
                sum_send[k, lo:hi] = (own + pair_recv[k, lo:hi].astype(F32)).astype(BF16)

        def ring_send(i):
            peer = (first + n + i) % n
            src = sum_send.at[k, :, block_rows(peer)]
            remote(tag + "ring1", tag + "ring1", src, ring1.at[k, first], at(peer, second)).start()

        relay = k == 1 and far > 0

        def ring1_near():
            if relay:
                for taps, way in relay_taps:
                    src = sum_send.at[k, taps, block_rows((first + n // 2) % n)]
                    dst = relayed.at[k, taps]
                    device = at((first + n + way) % n, second)
                    remote(tag + "ring1", tag + "relay", src, dst, device).start()
                for i in range(far - 1, 0, -1):
                    ring_send(i)
                    ring_send(-i)
            else:
                for i in offsets_of(n):
                    ring_send(i)

        def ring1_far():
            if relay:
                arrived(tag + "relay", relayed.at[k])
                for taps, way in relay_taps:
                    rows = block_rows((first + n + way * far) % n)
                    own = sum_send[k, taps, rows, :].astype(F32)
                    sum_send[k, taps, rows, :] = (own + relayed[k, taps].astype(F32)).astype(BF16)
                ring_send(far)
                ring_send(-far)

        def ring2_start():
            total = sum_send[k, :, pl.ds(own_block, block), :].astype(F32)
            near = [i for i in range(1, n) if not relay or i != n // 2]
            arrived(tag + "ring1", ring1.at[k, 0 : len(near)])
            for i in near:
                total = total + ring1[k, (first + i) % n].astype(F32)
            fold[0:TAPS] = total.astype(BF16)
            sorted_rows = matmul(q2[...], fold[...].reshape(TAP_ROWS * block, channels))
            ring2_send[k] = sorted_rows.astype(BF16).reshape(n, 2 * TAP_ROWS, channels)
            for i in offsets_of(n):
                peer = (second + i) % n
                src, dst = ring2_send.at[k, peer], ring2.at[k, second]
                remote(tag + "ring2", tag + "ring2", src, dst, at(first, peer)).start()

        def ring2_sum():
            total = ring2_send[k, second].astype(F32)
            arrived(tag + "ring2", ring2.at[k, 0 : n - 1])
            for i in range(1, n):
                total = total + ring2[k, (second + i) % n].astype(F32)
            return total[0 : 2 * TAPS + 6]

        def finish():
            sent(tag + "pair", pair_send.at[k])
            sent(tag + "ring1", sum_send.at[k, :, 0 : (n - 1) * block])
            sent(tag + "ring2", ring2_send.at[k, 0 : n - 1])

        return pair_start, pair_sum, ring1_near, ring1_far, ring2_start, ring2_sum, finish

    one_pair, one_sum, one_near, _, one_ring2, one_total, one_finish = scatter(0, g_1)
    two_pair, two_sum, two_near, two_far, two_ring2, two_total, two_finish = scatter(1, g_2)

    arrived("h_yg", halo.at[1:3])
    build(s_y, tb.at[0], halo.at[1], True, True)
    build(s_g, tb.at[3], halo.at[2], False, False)

    def weight_rows(c, f):
        return pl.ds(pl.multiple_of(c * half + f * block, block), block)

    arrived("gather_a", wa.at[0 : n - 1])
    for g in range(n):
        for t in range(TAPS):
            rows_f32[t * block + 2 * g : t * block + 2 * g + 2, :] = wa[g, t].astype(F32)
    mine = weight_rows(core, first)
    wr[:, mine, :] = rows_f32[...].astype(BF16).reshape(TAPS, block, channels)

    def weight_send(src, way, taps, slot):
        ref = wr.at[taps, weight_rows(core, src)]
        remote("gather_b", "gather_b", ref, ref, at((first + n + way) % n, second), slot).start()

    def share(f):
        ref = wr.at[:, weight_rows(core, f)]
        remote("share", "share", ref, ref, partner).start()

    def weights_from(f):
        arrived("gather_b", wr.at[:, weight_rows(core, f)], f)

    every = slice(0, TAPS)
    reach = range(far, 0, -1) if far > 0 else [1]
    for i in reach:
        weight_send(first, i, every, first)
        if far > 0:
            weight_send(first, -i, every, first)
    share(first)

    for t in range(TAPS):
        weight_terms(g_1, s_y, tb.at[3], False, t)
    arrived("h_a2", halo.at[0])
    build(s_a, tf.at[1], halo.at[0], True, True)

    @when(is_last)
    def _():
        for t in range(TAPS):
            weight_terms(g_1, s_a, gc.at[1], True, t)

    one_pair(0)

    opposite = (first + n // 2) % n
    if far > 0:
        for way in (1, -1):
            origin = (first + n + way * far) % n
            weights_from(origin)
            taps = slice(0, SPLIT) if way > 0 else slice(SPLIT, TAPS)
            receiver = (first + n - way) % n
            slot = origin if way > 0 else receiver
            weight_send(origin, -way, taps, slot)
            share(origin)
        for i in range(1, far):
            for way in (1, -1):
                origin = (first + n + way * i) % n
                weights_from(origin)
                share(origin)
        arrived("gather_b", wr.at[0:SPLIT, weight_rows(core, opposite)], opposite)
        arrived("gather_b", wr.at[SPLIT:TAPS, weight_rows(core, opposite)], first)
    else:
        weights_from(opposite)
    share(opposite)
    one_sum()
    one_near()
    arrived("share", wr.at[:, pl.ds(other_half, half)])

    load_mid.wait()
    r1[...] = as_tile(flat32(tb.at[1]) - conv(s_y))

    @when(has_prev)
    def _():
        remote("x_back_row", "h_r", r1.at[edge_row], halo.at[6], partner).start()
        remote("x_back_row", "h_y", r1.at[edge_row], halo.at[4], behind_partner).start()
        remote("x_back", "x_yy", r1, yy.at[0], behind).start()

    dx1[...] = cot_rebuilt(tb.at[2], s_y, s_g)

    @when(has_prev)
    def _():
        remote("x_back_row", "h_g", dx1.at[edge_row], halo.at[5], behind_partner).start()
        remote("x_back", "x_gc", dx1, gc.at[1], behind).start()

        arrived("h_r", halo.at[6])
        build(s_r, r1, halo.at[6], True, True)
        for part, (lo, hi) in enumerate(GROUPS[1]):
            for t in range(lo, hi):
                weight_terms(g_2, s_r, dx1, False, t)
            two_pair(part)

    load_a1.wait()
    n2[...] = as_tile(flat32(tf.at[0]) + conv(s_a))

    @when(has_next)
    def _():
        remote("x_ahead_row", "h_p", n2.at[edge_row], halo.at[3], ahead_partner).start()
        remote("x_ahead", "x_pp", n2, pp.at[1], ahead).start()

    @when(is_last)
    def _():
        yy[1] = n2[...]

    @when(has_prev)
    def _():
        two_sum()
        two_near()

    one_ring2()

    @when(has_prev)
    def _():
        two_far()

    arrived("h_y", halo.at[4])

    @when(has_next)
    def _():
        arrived("x_yy", yy)

    build(s_y2, yy.at[0], halo.at[4], True, True)
    out_b[...] = as_tile(flat32(yy.at[1]) - conv(s_y2))
    copy("bo", out_b, bwd_out.at[0]).start()
    copy("bo", yy.at[0], bwd_out.at[1]).start()

    arrived("h_p", halo.at[3])

    @when(has_prev)
    def _():
        arrived("x_pp", pp)

    build(s_p, pp.at[1], halo.at[3], True, True)
    out_a[...] = as_tile(flat32(pp.at[0]) + conv(s_p))
    copy("fo", pp.at[1], fwd_out.at[0]).start()
    copy("fo", out_a, fwd_out.at[1]).start()

    @when(has_prev)
    def _():
        two_ring2()

    arrived("h_g", halo.at[5])

    @when(has_next)
    def _():
        arrived("x_gc", gc)

    build(s_g2, gc.at[1], halo.at[5], False, False)
    out_c[...] = cot_rebuilt(gc.at[0], s_y2, s_g2)
    copy("bo", gc.at[1], bwd_out.at[2]).start()
    copy("bo", out_c, bwd_out.at[3]).start()
    rows_f32[0 : 2 * TAPS + 6, :] = one_total()

    @when(has_prev)
    def _():
        res2[...] = two_total()
        remote("x_fin", "x_fin", res2, fin, behind).start()

    @when(has_next)
    def _():
        arrived("x_fin", fin)
        rows_f32[0 : 2 * TAPS + 6, :] = rows_f32[0 : 2 * TAPS + 6, :] + fin[...]

    for t in range(TAPS):
        grad_out[t] = rows_f32[2 * t : 2 * t + 2, :] * scale

    sent("gather_a", wa.at[0 : n - 1])
    sent("gather_b", wr.at[:, 0 : (n - 1) * block])
    sent("share", wr.at[:, pl.ds(other_half, half)])
    sent("halo", halo.at[0:3])
    one_finish()

    @when(has_prev)
    def _():
        sent("x_back", tb)
        sent("x_back_row", halo.at[0:3])
        sent("x_fin", fin)
        two_finish()

    @when(has_next)
    def _():
        sent("x_ahead", tf)
        sent("x_ahead_row", halo.at[0])

    @when(is_first)
    def _():
        sent("edge", halo.at[0])

    @when(is_last)
    def _():
        sent("edge", halo.at[0:2])

    copy("fo", fwd_out, fwd_out).wait()
    copy("bo", bwd_out, bwd_out).wait()


def fused(n, segments, scale, fwd, bwd, fresh, top, w):
    height, width, channels = fwd.shape[1:]
    tile = (height, width, channels)
    shifted = (3, height + 2, width, channels)
    half = channels // 2
    block = 2 * n
    n_send, n_recv, n_local = plan(n)[3:]
    square = (channels, channels)
    mixed = (block * TAP_ROWS, block * TAP_ROWS)
    v = pltpu.VMEM
    scratch = [
        v((2, *tile), BF16),
        v((4, *tile), BF16),
        v((2, *tile), BF16),
        v((2, *tile), BF16),
        v((2, *tile), BF16),
        v((7, width, channels), BF16),
        v(tile, BF16),
        v(tile, BF16),
        v(tile, BF16),
        v(tile, BF16),
        v(tile, BF16),
        v(tile, BF16),
        *[v(shifted, BF16)] * 7,
        v((n, TAPS, 2, channels), BF16),
        v((TAPS, channels, channels), BF16),
        v(square, BF16),
        v(square, BF16),
        v(mixed, BF16),
        v((max(TAPS * block, 2 * TAPS + 6), channels), F32),
        v((TAPS, channels, channels), F32),
        v((TAPS, channels, channels), F32),
        v((2, TAPS, half, channels), BF16),
        v((2, TAPS, half, channels), BF16),
        v((2, TAPS, half, channels), BF16),
        v((2, TAPS, block, channels), BF16),
        v((2, n, TAPS, block, channels), BF16),
        v((TAP_ROWS, block, channels), BF16),
        v((2, n, 2 * TAP_ROWS, channels), BF16),
        v((2, n, 2 * TAP_ROWS, channels), BF16),
        v((2 * TAPS + 6, channels), F32),
        v((2 * TAPS + 6, channels), F32),
        pltpu.SemaphoreType.DMA((n_send,)),
        pltpu.SemaphoreType.DMA((n_recv,)),
        pltpu.SemaphoreType.DMA((n_local,)),
    ]
    return pl.pallas_call(
        functools.partial(kernel, n, segments, height, width, channels, scale),
        out_shape=(
            jax.ShapeDtypeStruct((2, *tile), BF16),
            jax.ShapeDtypeStruct((4, *tile), BF16),
            jax.ShapeDtypeStruct((TAPS, 2, channels), F32),
        ),
        in_specs=[pl.BlockSpec(memory_space=pltpu.HBM)] * 5,
        out_specs=(
            pl.BlockSpec(memory_space=pl.ANY),
            pl.BlockSpec(memory_space=pl.ANY),
            pl.BlockSpec(memory_space=pltpu.VMEM),
        ),
        scratch_shapes=scratch,
        compiler_params=pltpu.CompilerParams(collective_id=0, has_side_effects=True, vmem_limit_bytes=44 << 20),
        name="coupling",
    )(*[pltpu.with_memory_space_constraint(x, pltpu.HBM) for x in (fwd, bwd, fresh, top, w)])


def place_kernel(a, b, c, a_out, b_out, c_out, sems):
    copies = [
        pltpu.make_async_copy(src, dst, sems.at[i])
        for i, (src, dst) in enumerate(((b, b_out), (a, a_out), (c, c_out)))
    ]
    for c in copies:
        c.start()
    for c in copies:
        c.wait()


def placed(arrays):
    return pl.pallas_call(
        place_kernel,
        out_shape=tuple(jax.ShapeDtypeStruct(x.shape, x.dtype) for x in arrays),
        in_specs=[pl.BlockSpec(memory_space=pl.ANY)] * 3,
        out_specs=(pl.BlockSpec(memory_space=pl.ANY),) * 3,
        scratch_shapes=[pltpu.SemaphoreType.DMA((3,))],
        compiler_params=pltpu.CompilerParams(vmem_limit_bytes=8 << 20),
        name="place",
    )(*arrays)


def shards(segments, tiles, fwd_in, bwd_in, fresh, top_cot, conv_weight):
    height, width, channels = fwd_in.shape[3:]
    n = math.isqrt(tiles // 2)
    scale = (2.0 * tiles * height * width) ** (-0.5)
    weight = conv_weight[0].transpose(1, 0, 2)
    results = fused(
        n, segments, scale, fwd_in[:, 0, 0], bwd_in[:, 0, 0], fresh[:, 0], top_cot[:, 0], weight
    )
    forward, message, grad = placed(results)
    return forward[:, None, None], message[:, None, None], grad.transpose(1, 0, 2)[None]


def solution(mesh):
    segments = mesh.shape["segment"]
    tiles = mesh.shape["dp"]
    streams = P(None, "segment", "dp", None, None, None)
    halves = P(None, "dp", None, None, None)
    weights = P("segment", "dp", None, None)
    return jax.shard_map(
        functools.partial(shards, segments, tiles),
        mesh=mesh,
        in_specs=(streams, streams, halves, halves, weights),
        out_specs=(streams, streams, weights),
        check_vma=False,
    )
```
